128 devices in a mesh: owner: 32 (over x, z, core), view: 4 (over y).
Axes of the slice: x: 4, y: 4, z: 4, core: 2. Of those that a mesh axis runs over, the one named last changes fastest.
Arguments:
- estimate: float32 [512, 128, 512], P('owner'), may hold values from 0.5 to 2
- axial_views: float32 [4, 512, 128, 512], P('view', 'owner'), may hold values from 0.3 to 3
- lateral_views: float32 [4, 512, 128, 512], P('view', 'owner'), may hold values from 0.3 to 3
- psf_axial: float32 [4, 3, 33], P('view'), may hold values from 0.05 to 1
- psf_lateral: float32 [4, 3, 33], P('view'), may hold values from 0.05 to 1
- coverage: int32 [32, 4, 8], P('owner'), may hold values from 0 to 1, as said below
Outputs:
- deconvolved: float32 [512, 128, 512], P('owner')
The draws below stay inside these ranges and needn't reach their ends.
Inputs may be any that keep to these rules, and one draw needn't show every extreme that they name: `coverage`: each block is covered by 2 to 6 views; some block by exactly 6 and some by exactly 2.
All inputs are finite; a program needn't handle non-finite values.
Results may differ from the reference program's by a relative error of at most 0.0001.
Values sent between devices are 32-bit elements; how exact they have to be, the bound alone decides.
No kernel may reach another device: no remote copies, remote signals or barrier semaphores. Data moves between devices by JAX's collectives and lax.ppermute only.
A program may use at most 128 MiB of HBM per device.

```python
import math
import jax
import jax.numpy as jnp
from jax import lax

BZ = 16
Y = 128
VA = 4
VL = 4
NBX = 4
ITERS = 2
Z = 512
X = 512
VIEWS = 8
KW = 33
N_OWNER = 32


def draw_coverage(key, part):
    count_key, score_key = jax.random.split(jax.random.fold_in(key, 7))
    counts = jax.random.randint(count_key, (N_OWNER, NBX), 2, 7)
    counts = counts.at[0, 0].set(6).at[0, 1].set(2)
    scores = jax.random.randint(score_key, (N_OWNER, NBX, VIEWS), 0, 4096) * VIEWS + jnp.arange(VIEWS)
    ordering = jnp.argsort(scores, axis=-1)
    ranking = jnp.argsort(ordering, axis=-1)
    return (ranking < counts[:, :, None]).astype(jnp.int32)


def levels(stream_key, shape, cuts, low, high):
    level, own = 1.0, jax.random.fold_in(stream_key, 6)
    for dim, shards_of in cuts:
        draws = jnp.exp(jax.random.uniform(jax.random.fold_in(own, dim), (shards_of,), jnp.float32, low / len(cuts), high / len(cuts)))
        level = level * jnp.repeat(draws, shape[dim] // shards_of).reshape([-1 if axis == dim else 1 for axis in range(len(shape))])
    return level


def setup_inputs(seed: int = 0) -> dict:
    splits = jax.random.split(jax.random.key(seed), 7)
    estimate = jnp.clip(jnp.exp(math.log(2.0) - 1.3862944 * jax.random.uniform(splits[0], (Z, Y, X), jnp.float32) ** levels(splits[0], (Z, Y, X), ((0, 32),), -0.2, 0.2)), 0.5, 2.0)
    axial_views = jnp.clip(jnp.exp(math.log(3.0) - 2.3025851 * jax.random.uniform(splits[1], (VA, Z, Y, X), jnp.float32) ** levels(splits[1], (VA, Z, Y, X), ((0, 4), (1, 32)), -0.2, 0.2)), 0.3, 3.0)
    lateral_views = jnp.clip(jnp.exp(math.log(3.0) - 2.3025851 * jax.random.uniform(splits[2], (VL, X, Y, Z), jnp.float32) ** levels(splits[2], (VL, X, Y, Z), ((0, 4), (1, 32)), -0.2, 0.2)), 0.3, 3.0)
    psf_axial = jnp.clip(jnp.exp(math.log(1.0) - 2.9957323 * jax.random.uniform(splits[3], (VA, 3, KW), jnp.float32) ** levels(splits[3], (VA, 3, KW), ((0, 4),), -0.2, 0.2)), 0.05, 1.0)
    psf_lateral = jnp.clip(jnp.exp(math.log(1.0) - 2.9957323 * jax.random.uniform(splits[4], (VL, 3, KW), jnp.float32) ** levels(splits[4], (VL, 3, KW), ((0, 4),), -0.2, 0.2)), 0.05, 1.0)
    coverage = draw_coverage(jax.random.fold_in(splits[6], 71), 0)
    return dict(estimate=estimate, axial_views=axial_views, lateral_views=lateral_views, psf_axial=psf_axial, psf_lateral=psf_lateral, coverage=coverage)


PRECISE = lax.Precision.HIGHEST


def band_matrix(kernel, block_width):
    rim_width = (kernel.shape[0] - 1) // 2
    row_index = jnp.arange(block_width + 2 * rim_width)[:, None]
    col_index = jnp.arange(block_width)[None, :]
    matches = (row_index - col_index)[:, :, None] == jnp.arange(kernel.shape[0])[None, None, :]
    return jnp.sum(jnp.where(matches, kernel, 0.0), axis=-1)


def along_last(volume, kernel):
    rim_width = (kernel.shape[0] - 1) // 2
    length = volume.shape[-1]
    block_width = min(128, length)
    blocks = volume.reshape(volume.shape[:-1] + (length // block_width, block_width))
    zero_rim = jnp.zeros(blocks.shape[:-2] + (1, rim_width), volume.dtype)
    left_rim = jnp.concatenate([zero_rim, blocks[..., :-1, block_width - rim_width:]], axis=-2)
    right_rim = jnp.concatenate([blocks[..., 1:, :rim_width], zero_rim], axis=-2)
    windows = jnp.concatenate([left_rim, blocks, right_rim], axis=-1)
    result = jnp.einsum("...bs,si->...bi", windows, band_matrix(kernel, block_width), precision=PRECISE)
    return result.reshape(volume.shape)


def blur_volume(volume, kernels):
    for axis_number in range(3):
        moved = jnp.moveaxis(volume, axis_number, -1)
        volume = jnp.moveaxis(along_last(moved, kernels[axis_number]), -1, axis_number)
    return volume


def edge_weights(kernel, length):
    rim_width = (kernel.shape[0] - 1) // 2
    source = jnp.arange(length)[:, None] + jnp.arange(kernel.shape[0])[None, :] - rim_width
    inside = (source >= 0) & (source < length)
    return jnp.sum(jnp.where(inside, kernel, 0.0), axis=-1)


def reference(estimate, axial_views, lateral_views, psf_axial, psf_lateral, coverage):
    psf_all = jnp.concatenate([psf_axial, psf_lateral], axis=0)
    kernel = psf_all / jnp.sum(psf_all, axis=-1, keepdims=True)
    flipped = kernel[..., ::-1]
    plane_count, line_count, column_count = estimate.shape
    view_total = psf_all.shape[0]
    block_rows = jnp.arange(plane_count) // BZ
    block_cols = jnp.arange(column_count) // (column_count // NBX)
    covered = coverage[block_rows][:, block_cols, :].astype(jnp.float32)
    cover_count = jnp.sum(coverage[block_rows][:, block_cols, :], axis=-1).astype(jnp.float32)
    for iteration in range(ITERS):
        log_total = jnp.zeros(estimate.shape, jnp.float32)
        for view_number in range(view_total):
            if view_number < VA:
                observed = axial_views[view_number]
            else:
                observed = jnp.transpose(lateral_views[view_number - VA], (2, 1, 0))
            blurred = blur_volume(estimate, kernel[view_number])
            quotient = observed / blurred
            back_sum = blur_volume(quotient, flipped[view_number])
            scale_sum = (edge_weights(flipped[view_number, 0], plane_count)[:, None, None]
                         * edge_weights(flipped[view_number, 1], line_count)[None, :, None]
                         * edge_weights(flipped[view_number, 2], column_count)[None, None, :])
            log_total = log_total + covered[:, None, :, view_number] * jnp.log(back_sum / scale_sum)
        estimate = estimate * jnp.exp(log_total / cover_count[:, None, :])
    return estimate
```

```python
import functools

import jax
import jax.numpy as jnp
from jax import lax
from jax.experimental import pallas as pl
from jax.experimental.pallas import tpu as pltpu
from jax.sharding import PartitionSpec as P

ITERS = 2
VA = 4
RIM = 16
BF = jnp.bfloat16
F32 = jnp.float32

COLS = 8
GROUPS = [list(range(8 * g, 8 * g + 8)) for g in range(4)]
Z_UP = [(8 * x + k, 8 * x + 8 + k) for x in range(3) for k in range(8)]
Z_DOWN = [(b, a) for a, b in Z_UP]
X_UP = [(8 * x + k, 8 * x + k + 1) for x in range(4) for k in range(7)]
X_DOWN = [(b, a) for a, b in X_UP]
V_UP = [(i, (i + 1) % 4) for i in range(4)]
V_DOWN = [(b, a) for a, b in V_UP]


def lateral_round(t):
    return [
        (4 * k + r, ((r + t + k // 2) % 4) * 8 + k) for k in range(8) for r in range(4)
    ]


def split(value):
    hi = value.astype(BF)
    lo = (value - hi.astype(F32)).astype(BF)
    return hi, lo


def band(kernel, length, extended):
    rim = RIM if extended else 0
    taps = kernel.shape[-1]
    row = jnp.arange(length)[:, None]
    col = jnp.arange(length + 2 * rim)[None, :]
    offset = col - row + (RIM - rim)
    hit = offset[:, :, None] == jnp.arange(taps)[None, None, :]
    return jnp.sum(jnp.where(hit, kernel[..., None, None, :], 0.0), axis=-1)


def edge_weights(kernel, positions, total):
    source = positions[:, None] + jnp.arange(kernel.shape[-1])[None, :] - RIM
    inside = (source >= 0) & (source < total)
    return jnp.sum(jnp.where(inside, kernel[..., None, :], 0.0), axis=-1)


def split_matrix(value):
    hi = lax.reduce_precision(value, 8, 7)
    return hi.astype(BF), (value - hi).astype(BF)


def left_form(matrix):
    hi, lo = split_matrix(matrix)
    return jnp.concatenate([hi, lo, hi], axis=-1)


def right_form(matrix):
    hi, lo = split_matrix(matrix)
    return jnp.concatenate([hi, lo, hi], axis=-2)


def dot(a, b):
    return lax.dot_general(a, b, (((1,), (0,)), ((), ())), preferred_element_type=F32)


def conv_rows(matrix, data):
    hi, lo = split(data)
    return dot(matrix, jnp.concatenate([hi, hi, lo], axis=0))


def conv_lanes(data, matrix):
    hi, lo = split(data)
    return dot(jnp.concatenate([hi, hi, lo], axis=1), matrix)


def xy_planes(load, mx, my, planes, finish):
    for p in range(0, planes, 2):
        pair = jnp.concatenate([load(p), load(p + 1)], axis=1)
        mid = conv_rows(mx, pair)
        both = jnp.concatenate([mid[:, :128], mid[:, 128:]], axis=0)
        done = conv_lanes(both, my)
        half = done.shape[0] // 2
        finish(p, done[:half])
        finish(p + 1, done[half:])


def forward_kernel(mz_ref, mx_ref, my_ref, f_ref, zb_ref, za_ref, xl_ref, xr_ref, obs_ref, q_ref, w_ref):
    depth, width = f_ref.shape[0], f_ref.shape[1]
    wide = width + 2 * RIM

    @pl.when(pl.program_id(0) == 0)
    def _():
        mz = mz_ref[...]
        w_flat = w_ref.reshape(depth * wide, 128)
        f_flat = f_ref.reshape(depth * width, 128)
        b_flat = zb_ref.reshape(RIM * width, 128)
        a_flat = za_ref.reshape(RIM * width, 128)

        def column(x):
            return jnp.concatenate(
                [
                    b_flat[pl.ds(x, RIM, stride=width), :],
                    f_flat[pl.ds(x, depth, stride=width), :],
                    a_flat[pl.ds(x, RIM, stride=width), :],
                ],
                axis=0,
            )

        def body(i, _):
            x = 2 * i
            out = conv_rows(mz, jnp.concatenate([column(x), column(x + 1)], axis=1))
            w_flat[pl.ds(x + RIM, depth, stride=wide), :] = out[:, :128]
            w_flat[pl.ds(x + 1 + RIM, depth, stride=wide), :] = out[:, 128:]
            return 0

        lax.fori_loop(0, width // 2, body, 0)
        long = depth + 2 * RIM
        for side, base in ((xl_ref, 0), (xr_ref, RIM + width)):
            s_flat = side.reshape(long * RIM, 128)

            def edge(i, _):
                x = 2 * i
                pair = jnp.concatenate(
                    [s_flat[pl.ds(x, long, stride=RIM), :], s_flat[pl.ds(x + 1, long, stride=RIM), :]],
                    axis=1,
                )
                out = conv_rows(mz, pair)
                w_flat[pl.ds(x + base, depth, stride=wide), :] = out[:, :128]
                w_flat[pl.ds(x + 1 + base, depth, stride=wide), :] = out[:, 128:]
                return 0

            lax.fori_loop(0, RIM // 2, edge, 0)

    planes = obs_ref.shape[0]
    first = pl.program_id(0) * planes

    def finish(p, blurred):
        q_ref[p] = obs_ref[p] / blurred

    xy_planes(lambda p: w_ref[first + p], mx_ref[...], my_ref[...], planes, finish)


def back_z_kernel(mz_ref, q_ref, zb_ref, za_ref, r_ref):
    depth, width = q_ref.shape[0], q_ref.shape[1]
    q_flat = q_ref.reshape(depth * width, 128)
    b_flat = zb_ref.reshape(RIM * width, 128)
    a_flat = za_ref.reshape(RIM * width, 128)
    r_flat = r_ref.reshape(depth * width, 128)
    mz = mz_ref[...]

    def column(x):
        return jnp.concatenate(
            [
                b_flat[pl.ds(x, RIM, stride=width), :],
                q_flat[pl.ds(x, depth, stride=width), :],
                a_flat[pl.ds(x, RIM, stride=width), :],
            ],
            axis=0,
        )

    for x in range(0, width, 2):
        out = conv_rows(mz, jnp.concatenate([column(x), column(x + 1)], axis=1))
        r_flat[pl.ds(x, depth, stride=width), :] = out[:, :128]
        r_flat[pl.ds(x + 1, depth, stride=width), :] = out[:, 128:]


def back_xy_kernel(me_ref, w_ref, mx_ref, my_ref, r_ref, xl_ref, xr_ref, *rest):
    acc_ref, l_ref = rest if len(rest) == 2 else (None, rest[0])
    planes = r_ref.shape[0]
    me = me_ref[0]
    weight = w_ref[pl.program_id(0)]

    def load(p):
        return jnp.concatenate([xl_ref[p], r_ref[p], xr_ref[p]], axis=0)

    def finish(p, back):
        term = weight * jnp.log(back)
        for quarter in range(4):
            slot = lax.rem(quarter - me + 4, 4)
            part = term[quarter * 16 : quarter * 16 + 16]
            if acc_ref is not None:
                part = part + acc_ref[slot, p]
            l_ref[slot, p] = part

    xy_planes(load, mx_ref[...], my_ref[...], planes, finish)


def whole(shape):
    return pl.BlockSpec(shape, lambda i: (0,) * len(shape))


def forward(mz, mx, my, f, zb, za, xl, xr, obs):
    depth, width, lines = f.shape
    planes = 16
    moving = pl.BlockSpec((planes, width, lines), lambda i: (i, 0, 0))
    return pl.pallas_call(
        forward_kernel,
        grid=(depth // planes,),
        in_specs=[whole(v.shape) for v in (mz, mx, my, f, zb, za, xl, xr)] + [moving],
        out_specs=moving,
        out_shape=jax.ShapeDtypeStruct(obs.shape, F32),
        scratch_shapes=[pltpu.VMEM((depth, width + 2 * RIM, lines), F32)],
        cost_estimate=pl.CostEstimate(flops=10**10, bytes_accessed=2 * 10**7, transcendentals=0),
        name="forward",
    )(mz, mx, my, f, zb, za, xl, xr, obs)


def back_z(mz, q, zb, za):
    depth, width, lines = q.shape
    group = 8
    part = pl.BlockSpec((depth, group, lines), lambda i: (0, i, 0))
    rim = pl.BlockSpec((RIM, group, lines), lambda i: (0, i, 0))
    return pl.pallas_call(
        back_z_kernel,
        grid=(width // group,),
        in_specs=[whole(mz.shape), part, rim, rim],
        out_specs=part,
        out_shape=jax.ShapeDtypeStruct(q.shape, F32),
        cost_estimate=pl.CostEstimate(flops=3 * 10**9, bytes_accessed=10**7, transcendentals=0),
        name="back_z",
    )(mz, q, zb, za)


def back_xy(me, weight, mx, my, r, xl, xr, acc=None):
    depth, width, lines = r.shape
    planes = 16
    smem = pl.BlockSpec(memory_space=pltpu.SMEM)
    part = pl.BlockSpec((planes, width, lines), lambda i: (i, 0, 0))
    rim = pl.BlockSpec((planes, RIM, lines), lambda i: (i, 0, 0))
    out = pl.BlockSpec((4, planes, width // 4, lines), lambda i: (0, i, 0, 0))
    args = [me, weight, mx, my, r, xl, xr] + ([] if acc is None else [acc])
    return pl.pallas_call(
        back_xy_kernel,
        grid=(depth // planes,),
        in_specs=[smem, smem, whole(mx.shape), whole(my.shape), part, rim, rim]
        + ([] if acc is None else [out]),
        out_specs=out,
        out_shape=jax.ShapeDtypeStruct((4, depth, width // 4, lines), F32),
        cost_estimate=pl.CostEstimate(flops=5 * 10**9, bytes_accessed=10**7, transcendentals=10**6),
        name="back_xy",
    )(*args)


def gather_quarters(quarter, half):
    below = lax.ppermute(quarter, "view", V_UP)
    above = lax.ppermute(quarter, "view", V_DOWN)
    first = lax.ppermute(below[:half], "view", V_UP)
    second = lax.ppermute(above[half:], "view", V_DOWN)
    return quarter, above, jnp.concatenate([first, second], axis=0), below


def scatter_quarters(parts):
    half = parts.shape[1] // 2
    first = lax.ppermute(parts[2, :half], "view", V_UP)
    second = lax.ppermute(parts[2, half:], "view", V_DOWN)
    up = jnp.concatenate([parts[1, :half] + first, parts[1, half:]], axis=0)
    down = jnp.concatenate([parts[3, :half], parts[3, half:] + second], axis=0)
    return parts[0] + lax.ppermute(up, "view", V_UP) + lax.ppermute(down, "view", V_DOWN)


def z_rims(block):
    before = lax.ppermute(block[-RIM:], "owner", Z_UP)
    after = lax.ppermute(block[:RIM], "owner", Z_DOWN)
    return before, after


def x_rims(right_edge, left_edge):
    left = lax.ppermute(right_edge, "owner", X_UP)
    right = lax.ppermute(left_edge, "owner", X_DOWN)
    return left, right


def local(estimate, axial_views, lateral_views, psf_axial, psf_lateral, coverage):
    slab, lines, columns = estimate.shape
    owner = lax.axis_index("owner")
    me = lax.axis_index("view")
    k = owner % 8
    z_chip = owner // 8
    width = columns // COLS
    depth = 8 * slab

    turned = estimate.transpose(0, 2, 1).reshape(slab, COLS, 4, width // 4, lines)
    mine = lax.dynamic_index_in_dim(turned, me, 2, keepdims=False).reshape(slab, -1, lines)
    quarter = lax.all_to_all(
        mine, "owner", split_axis=1, concat_axis=0, axis_index_groups=GROUPS, tiled=True
    )

    axial = lax.all_to_all(
        axial_views[0].transpose(0, 2, 1),
        "owner",
        split_axis=1,
        concat_axis=0,
        axis_index_groups=GROUPS,
        tiled=True,
    )
    chunks = lateral_views[0].transpose(2, 0, 1).reshape(4, depth, slab, lines)
    lateral = jnp.zeros((depth, width, lines), F32)
    for t in range(4):
        target = (owner % 4 + t + z_chip) % 4
        piece = lax.dynamic_index_in_dim(chunks, target, 0, keepdims=False)
        piece = lax.ppermute(piece, "owner", lateral_round(t))
        source = (z_chip - t - k // 2) % 4
        lateral = lax.dynamic_update_slice_in_dim(lateral, piece, source * slab, axis=1)

    cover = jnp.repeat(coverage[0].astype(F32), 2, axis=0)
    cover = lax.all_to_all(
        cover, "owner", split_axis=0, concat_axis=0, axis_index_groups=GROUPS, tiled=True
    )
    count = jnp.sum(cover, axis=-1)
    weight_axial = lax.dynamic_index_in_dim(cover, me, 1, keepdims=False)
    weight_lateral = lax.dynamic_index_in_dim(cover, VA + me, 1, keepdims=False)

    taps = jnp.concatenate([psf_axial, psf_lateral], axis=0)
    taps = taps / jnp.sum(taps, axis=-1, keepdims=True)
    flipped = taps[..., ::-1]
    z_at = z_chip * depth + jnp.arange(depth)
    x_at = k * width + jnp.arange(width)
    y_at = jnp.arange(lines)
    ahead_z = left_form(band(taps[:, 0], depth, True))
    ahead_x = left_form(band(taps[:, 2], width, True))
    ahead_y = right_form(jnp.swapaxes(band(taps[:, 1], lines, False), 1, 2))
    wz = edge_weights(flipped[:, 0], z_at, 4 * depth)
    wx = edge_weights(flipped[:, 2], x_at, columns)
    wy = edge_weights(flipped[:, 1], y_at, lines)
    back_mz = left_form(band(flipped[:, 0], depth, True) / wz[:, :, None])
    back_mx = left_form(band(flipped[:, 2], width, True) / wx[:, :, None])
    back_my = right_form(
        jnp.swapaxes(band(flipped[:, 1], lines, False) / wy[:, :, None], 1, 2)
    )
    me_arr = me[None].astype(jnp.int32)

    for iteration in range(ITERS):
        pieces = gather_quarters(quarter, depth // 2)
        block = jnp.zeros((depth, width, lines), F32)
        for d in range(4):
            at = ((me + d) % 4) * (width // 4)
            block = lax.dynamic_update_slice_in_dim(block, pieces[d], at, axis=1)
        before, after = z_rims(block)
        long_right = jnp.concatenate(
            [before[:, -RIM:], block[:, -RIM:], after[:, -RIM:]], axis=0
        )
        long_left = jnp.concatenate(
            [before[:, :RIM], block[:, :RIM], after[:, :RIM]], axis=0
        )
        left, right = x_rims(long_right, long_left)
        logs = None
        for number, (obs, weight) in enumerate(
            ((axial, weight_axial), (lateral, weight_lateral))
        ):
            quotient = forward(
                ahead_z[number], ahead_x[number], ahead_y[number],
                block, before, after, left, right, obs,
            )
            rz = back_z(back_mz[number], quotient, *z_rims(quotient))
            logs = back_xy(
                me_arr, weight, back_mx[number], back_my[number],
                rz, *x_rims(rz[:, -RIM:], rz[:, :RIM]), acc=logs,
            )
        total = scatter_quarters(logs)
        slabs = total.reshape(8, slab, width // 4, lines) / count[:, None, None, None]
        quarter = quarter * jnp.exp(slabs.reshape(quarter.shape))

    slabs = lax.all_to_all(
        quarter, "owner", split_axis=0, concat_axis=1, axis_index_groups=GROUPS, tiled=True
    )
    slabs = slabs.reshape(slab, COLS, width // 4, lines)
    pieces = gather_quarters(slabs, slab // 2)
    result = jnp.zeros((slab, COLS, 4, width // 4, lines), F32)
    for d in range(4):
        result = lax.dynamic_update_index_in_dim(result, pieces[d], (me + d) % 4, axis=2)
    return result.reshape(slab, columns, lines).transpose(0, 2, 1)


def solution(mesh):
    in_specs = (
        P("owner", None, None),
        P("view", "owner", None, None),
        P("view", "owner", None, None),
        P("view", None, None),
        P("view", None, None),
        P("owner", None, None),
    )
    out_specs = P("owner", None, None)
    return jax.shard_map(local, mesh=mesh, in_specs=in_specs, out_specs=out_specs, check_vma=False)
```

```python
import functools

import jax
import jax.numpy as jnp
from jax import lax
from jax.experimental import pallas as pl
from jax.experimental.pallas import tpu as pltpu
from jax.sharding import PartitionSpec as P

ITERS = 2
VA = 4
RIM = 16
UNROLL = 4
BF = jnp.bfloat16
F32 = jnp.float32

COLS = 8
GROUPS = [list(range(8 * g, 8 * g + 8)) for g in range(4)]
Z_UP = [(8 * x + k, 8 * x + 8 + k) for x in range(3) for k in range(8)]
Z_DOWN = [(b, a) for a, b in Z_UP]
X_UP = [(8 * x + k, 8 * x + k + 1) for x in range(4) for k in range(7)]
X_DOWN = [(b, a) for a, b in X_UP]
V_UP = [(i, (i + 1) % 4) for i in range(4)]
V_DOWN = [(b, a) for a, b in V_UP]


def lateral_round(t):
    return [
        (4 * k + r, ((r + t + k // 2) % 4) * 8 + k) for k in range(8) for r in range(4)
    ]


def split(value):
    hi = value.astype(BF)
    lo = (value - hi.astype(F32)).astype(BF)
    return hi, lo


def band(kernel, length, extended):
    rim = RIM if extended else 0
    taps = kernel.shape[-1]
    row = jnp.arange(length)[:, None]
    col = jnp.arange(length + 2 * rim)[None, :]
    offset = col - row + (RIM - rim)
    hit = offset[:, :, None] == jnp.arange(taps)[None, None, :]
    return jnp.sum(jnp.where(hit, kernel[..., None, None, :], 0.0), axis=-1)


def edge_weights(kernel, positions, total):
    source = positions[:, None] + jnp.arange(kernel.shape[-1])[None, :] - RIM
    inside = (source >= 0) & (source < total)
    return jnp.sum(jnp.where(inside, kernel[..., None, :], 0.0), axis=-1)


def split_matrix(value):
    hi = lax.reduce_precision(value, 8, 7)
    return hi.astype(BF), (value - hi).astype(BF)


def left_form(matrix):
    hi, lo = split_matrix(matrix)
    return jnp.concatenate([hi, lo, hi], axis=-1)


def right_form(matrix):
    hi, lo = split_matrix(matrix)
    return jnp.concatenate([hi, lo, hi], axis=-2)


def dot(a, b):
    return lax.dot_general(a, b, (((1,), (0,)), ((), ())), preferred_element_type=F32)


def conv_rows(matrix, data):
    hi, lo = split(data)
    return dot(matrix, jnp.concatenate([hi, hi, lo], axis=0))


def conv_lanes(data, matrix):
    hi, lo = split(data)
    return dot(jnp.concatenate([hi, hi, lo], axis=1), matrix)


def xy_planes(load, mx, my, planes, mid_ref, finish):
    group = 2 * UNROLL
    steps = planes // group

    def along_x(i):
        for u in range(0, group, 2):
            p = group * i + u
            mid = conv_rows(mx, jnp.concatenate([load(p), load(p + 1)], axis=1))
            half = mid.shape[0]
            slot = lax.rem(i, 2)
            mid_ref[slot, u * half : (u + 1) * half] = mid[:, :128]
            mid_ref[slot, (u + 1) * half : (u + 2) * half] = mid[:, 128:]

    def along_y(i):
        done = conv_lanes(mid_ref[lax.rem(i, 2)], my)
        half = done.shape[0] // group
        for u in range(group):
            finish(group * i + u, done[u * half : (u + 1) * half])

    def body(i, _):
        along_y(i - 1)
        along_x(i)
        return 0

    along_x(0)
    lax.fori_loop(1, steps, body, 0)
    along_y(steps - 1)


def z_columns(load, mz, columns, store):
    def body(i, _):
        for u in range(UNROLL):
            x = 2 * (UNROLL * i + u)
            out = conv_rows(mz, jnp.concatenate([load(x), load(x + 1)], axis=1))
            store(x, out[:, :128])
            store(x + 1, out[:, 128:])
        return 0

    lax.fori_loop(0, columns // (2 * UNROLL), body, 0)


def each(count, step):
    def body(i, _):
        for u in range(UNROLL):
            step(UNROLL * i + u)
        return 0

    lax.fori_loop(0, count // UNROLL, body, 0)


def forward_kernel(
    mz_ref, mx_ref, my_ref, f_ref, zb_ref, za_ref, xl_ref, xr_ref, obs_ref,
    q_ref, first_ref, last_ref, e_ref, w_ref, mid_ref,
):
    depth, width = f_ref.shape[0], f_ref.shape[1]
    wide = width + 2 * RIM
    pitch = wide + 1
    part = width + 1
    mz = mz_ref[...]

    def middle(source, start):
        def step(z):
            e_ref[pl.ds((start + z) * pitch + RIM, width), :] = source[z]

        each(source.shape[0], step)

    def sides(z):
        e_ref[pl.ds(z * pitch, RIM), :] = xl_ref[z]
        e_ref[pl.ds(z * pitch + RIM + width, RIM), :] = xr_ref[z]

    middle(zb_ref, 0)
    middle(f_ref, RIM)
    middle(za_ref, RIM + depth)
    each(depth + 2 * RIM, sides)

    def load(x):
        return e_ref[pl.ds(x, depth + 2 * RIM, stride=pitch), :]

    def store(x, value):
        w_ref[pl.ds(x, depth, stride=pitch), :] = value

    z_columns(load, mz, wide, store)

    def finish(p, blurred):
        q_ref[pl.ds(p * part, width), :] = obs_ref[p] / blurred

    xy_planes(
        lambda p: w_ref[pl.ds(p * pitch, wide), :], mx_ref[...], my_ref[...], depth, mid_ref, finish
    )

    def edges(z):
        first_ref[z] = q_ref[pl.ds(z * part, width), :]
        last_ref[z] = q_ref[pl.ds((depth - RIM + z) * part, width), :]

    each(RIM, edges)


def back_z_kernel(mz_ref, q_ref, zb_ref, za_ref, r_ref, first_ref, last_ref, b_ref, a_ref):
    width = zb_ref.shape[1]
    part = width + 1
    depth = q_ref.shape[0] // part

    def rims(z):
        b_ref[pl.ds(z * part, width), :] = zb_ref[z]
        a_ref[pl.ds(z * part, width), :] = za_ref[z]

    each(RIM, rims)

    def load(x):
        return jnp.concatenate(
            [
                b_ref[pl.ds(x, RIM, stride=part), :],
                q_ref[pl.ds(x, depth, stride=part), :],
                a_ref[pl.ds(x, RIM, stride=part), :],
            ],
            axis=0,
        )

    def store(x, value):
        r_ref[pl.ds(x, depth, stride=part), :] = value

    z_columns(load, mz_ref[...], width, store)

    def edges(z):
        first_ref[z] = r_ref[pl.ds(z * part, RIM), :]
        last_ref[z] = r_ref[pl.ds(z * part + width - RIM, RIM), :]

    each(depth, edges)


def back_xy_kernel(me_ref, w_ref, mx_ref, my_ref, r_ref, xl_ref, xr_ref, *rest):
    acc_ref, l_ref, mid_ref = rest if len(rest) == 3 else (None, *rest)
    me = me_ref[0]
    depth = xl_ref.shape[0]
    part = r_ref.shape[0] // depth

    def load(p):
        return jnp.concatenate(
            [xl_ref[p], r_ref[pl.ds(p * part, part - 1), :], xr_ref[p]], axis=0
        )

    def finish(p, back):
        term = w_ref[lax.div(p, 16)] * jnp.log(back)
        for quarter in range(4):
            slot = lax.rem(quarter - me + 4, 4)
            piece = term[quarter * 16 : quarter * 16 + 16]
            if acc_ref is not None:
                piece = piece + acc_ref[slot, p]
            l_ref[slot, p] = piece

    xy_planes(load, mx_ref[...], my_ref[...], depth, mid_ref, finish)


def assemble_kernel(at_ref, *refs):
    *pieces, block_ref, first_ref, last_ref = refs
    depth, narrow = pieces[0].shape[0], pieces[0].shape[1]
    for number, piece in enumerate(pieces):
        at = pl.multiple_of(at_ref[number], narrow)

        def step(z):
            block_ref[z, pl.ds(at, narrow), :] = piece[z]

        each(depth, step)
    first_ref[...] = block_ref[:RIM]
    last_ref[...] = block_ref[depth - RIM :]


VMEM = pl.BlockSpec(memory_space=pltpu.VMEM)
SMEM = pl.BlockSpec(memory_space=pltpu.SMEM)


def params(mebibytes):
    return pltpu.CompilerParams(vmem_limit_bytes=mebibytes * 2**20)


def forward(mz, mx, my, f, zb, za, xl, xr, obs):
    depth, width, lines = f.shape
    rim = jax.ShapeDtypeStruct((RIM, width, lines), F32)
    pitch = width + 2 * RIM + 1
    return pl.pallas_call(
        forward_kernel,
        in_specs=[VMEM] * 9,
        out_specs=[VMEM] * 3,
        out_shape=[jax.ShapeDtypeStruct((depth * (width + 1), lines), F32), rim, rim],
        scratch_shapes=[
            pltpu.VMEM(((depth + 2 * RIM) * pitch, lines), F32),
            pltpu.VMEM((depth * pitch, lines), F32),
            pltpu.VMEM((2, 2 * UNROLL * width, lines), F32),
        ],
        compiler_params=params(20),
        cost_estimate=pl.CostEstimate(flops=10**10, bytes_accessed=2 * 10**7, transcendentals=0),
        name="forward",
    )(mz, mx, my, f, zb, za, xl, xr, obs)


def back_z(mz, q, zb, za):
    width, lines = zb.shape[1:]
    depth = q.shape[0] // (width + 1)
    rim = jax.ShapeDtypeStruct((depth, RIM, lines), F32)
    padded = pltpu.VMEM((RIM * (width + 1), lines), F32)
    return pl.pallas_call(
        back_z_kernel,
        in_specs=[VMEM] * 4,
        out_specs=[VMEM] * 3,
        out_shape=[jax.ShapeDtypeStruct(q.shape, F32), rim, rim],
        scratch_shapes=[padded, padded],
        compiler_params=params(12),
        cost_estimate=pl.CostEstimate(flops=3 * 10**9, bytes_accessed=10**7, transcendentals=0),
        name="back_z",
    )(mz, q, zb, za)


def back_xy(me, weight, mx, my, r, xl, xr, acc=None):
    depth, _, lines = xl.shape
    width = r.shape[0] // depth - 1
    args = [me, weight, mx, my, r, xl, xr] + ([] if acc is None else [acc])
    return pl.pallas_call(
        back_xy_kernel,
        in_specs=[SMEM, SMEM] + [VMEM] * (len(args) - 2),
        out_specs=VMEM,
        out_shape=jax.ShapeDtypeStruct((4, depth, width // 4, lines), F32),
        scratch_shapes=[pltpu.VMEM((2, 2 * UNROLL * width, lines), F32)],
        compiler_params=params(12),
        cost_estimate=pl.CostEstimate(flops=5 * 10**9, bytes_accessed=10**7, transcendentals=10**6),
        name="back_xy",
    )(*args)


def assemble(at, pieces):
    depth, narrow, lines = pieces[0].shape
    width = narrow * len(pieces)
    rim = jax.ShapeDtypeStruct((RIM, width, lines), F32)
    return pl.pallas_call(
        assemble_kernel,
        in_specs=[SMEM] + [VMEM] * len(pieces),
        out_specs=[VMEM] * 3,
        out_shape=[jax.ShapeDtypeStruct((depth, width, lines), F32), rim, rim],
        compiler_params=params(6),
        cost_estimate=pl.CostEstimate(flops=10**6, bytes_accessed=10**7, transcendentals=0),
        name="assemble",
    )(at.astype(jnp.int32), *pieces)


def gather_quarters(quarter, half):
    below = lax.ppermute(quarter, "view", V_UP)
    above = lax.ppermute(quarter, "view", V_DOWN)
    first = lax.ppermute(below[:half], "view", V_UP)
    second = lax.ppermute(above[half:], "view", V_DOWN)
    return quarter, above, jnp.concatenate([first, second], axis=0), below


def scatter_quarters(parts):
    half = parts.shape[1] // 2
    first = lax.ppermute(parts[2, :half], "view", V_UP)
    second = lax.ppermute(parts[2, half:], "view", V_DOWN)
    up = jnp.concatenate([parts[1, :half] + first, parts[1, half:]], axis=0)
    down = jnp.concatenate([parts[3, :half], parts[3, half:] + second], axis=0)
    return parts[0] + lax.ppermute(up, "view", V_UP) + lax.ppermute(down, "view", V_DOWN)


def to_blocks(value):
    return lax.all_to_all(
        value, "owner", split_axis=1, concat_axis=0, axis_index_groups=GROUPS, tiled=True
    )


def z_rims(first, last):
    before = lax.ppermute(last, "owner", Z_UP)
    after = lax.ppermute(first, "owner", Z_DOWN)
    return before, after


def x_rims(first, last):
    left = lax.ppermute(last, "owner", X_UP)
    right = lax.ppermute(first, "owner", X_DOWN)
    return left, right


def local(estimate, axial_views, lateral_views, psf_axial, psf_lateral, coverage):
    slab, lines, columns = estimate.shape
    owner = lax.axis_index("owner")
    me = lax.axis_index("view")
    k = owner % 8
    z_chip = owner // 8
    width = columns // COLS
    depth = 8 * slab

    turned = estimate.transpose(0, 2, 1).reshape(slab, COLS, 4, width // 4, lines)
    mine = lax.dynamic_index_in_dim(turned, me, 2, keepdims=False)
    cover = jnp.repeat(coverage[0].astype(F32), 2, axis=0)
    cover = jnp.pad(cover[:, None, :], ((0, 0), (0, width // 4 - 1), (0, lines - cover.shape[1])))
    mine = jnp.concatenate([mine, cover[None]], axis=0).reshape(slab + 1, -1, lines)
    axial_views, mine = lax.optimization_barrier((axial_views, mine))
    got = to_blocks(mine).reshape(8, slab + 1, width // 4, lines)
    axial_turned = axial_views[0].transpose(0, 2, 1)
    lateral_views, axial_turned, got = lax.optimization_barrier(
        (lateral_views, axial_turned, got)
    )
    axial = to_blocks(axial_turned)
    quarter = got[:, :slab].reshape(depth, width // 4, lines)
    cover = got[:, slab, 0, :8]

    chunks = lateral_views[0].transpose(2, 0, 1).reshape(4, depth, slab, lines)
    pieces, places = [], []
    for t in range(4):
        target = (owner % 4 + t + z_chip) % 4
        piece = lax.dynamic_index_in_dim(chunks, target, 0, keepdims=False)
        pieces.append(lax.ppermute(piece, "owner", lateral_round(t)))
        places.append(((z_chip - t - k // 2) % 4) * slab)
    lateral = assemble(jnp.stack(places), pieces)[0]

    count = jnp.sum(cover, axis=-1)
    weight_axial = lax.dynamic_index_in_dim(cover, me, 1, keepdims=False)
    weight_lateral = lax.dynamic_index_in_dim(cover, VA + me, 1, keepdims=False)

    taps = jnp.concatenate([psf_axial, psf_lateral], axis=0)
    taps = taps / jnp.sum(taps, axis=-1, keepdims=True)
    flipped = taps[..., ::-1]
    z_at = z_chip * depth + jnp.arange(depth)
    x_at = k * width + jnp.arange(width)
    y_at = jnp.arange(lines)
    ahead_z = left_form(band(taps[:, 0], depth, True))
    ahead_x = left_form(band(taps[:, 2], width, True))
    ahead_y = right_form(jnp.swapaxes(band(taps[:, 1], lines, False), 1, 2))
    wz = edge_weights(flipped[:, 0], z_at, 4 * depth)
    wx = edge_weights(flipped[:, 2], x_at, columns)
    wy = edge_weights(flipped[:, 1], y_at, lines)
    back_mz = left_form(band(flipped[:, 0], depth, True) / wz[:, :, None])
    back_mx = left_form(band(flipped[:, 2], width, True) / wx[:, :, None])
    back_my = right_form(
        jnp.swapaxes(band(flipped[:, 1], lines, False) / wy[:, :, None], 1, 2)
    )
    me_arr = me[None].astype(jnp.int32)

    for iteration in range(ITERS):
        pieces = gather_quarters(quarter, depth // 2)
        places = ((me + jnp.arange(4)) % 4) * (width // 4)
        block, first, last = assemble(places, pieces)
        before, after = z_rims(first, last)
        long_right = jnp.concatenate(
            [before[:, -RIM:], block[:, -RIM:], after[:, -RIM:]], axis=0
        )
        long_left = jnp.concatenate(
            [before[:, :RIM], block[:, :RIM], after[:, :RIM]], axis=0
        )
        left, right = x_rims(long_left, long_right)
        logs = None
        for number, (obs, weight) in enumerate(
            ((axial, weight_axial), (lateral, weight_lateral))
        ):
            quotient, first, last = forward(
                ahead_z[number], ahead_x[number], ahead_y[number],
                block, before, after, left, right, obs,
            )
            rz, low, high = back_z(back_mz[number], quotient, *z_rims(first, last))
            logs = back_xy(
                me_arr, weight, back_mx[number], back_my[number],
                rz, *x_rims(low, high), acc=logs,
            )
        total = scatter_quarters(logs)
        slabs = total.reshape(8, slab, width // 4, lines) / count[:, None, None, None]
        quarter = quarter * jnp.exp(slabs.reshape(quarter.shape))

    slabs = lax.all_to_all(
        quarter, "owner", split_axis=0, concat_axis=1, axis_index_groups=GROUPS, tiled=True
    )
    slabs = slabs.reshape(slab, COLS, width // 4, lines)
    pieces = gather_quarters(slabs, slab // 2)
    result = jnp.zeros((slab, COLS, 4, width // 4, lines), F32)
    for d in range(4):
        result = lax.dynamic_update_index_in_dim(result, pieces[d], (me + d) % 4, axis=2)
    return result.reshape(slab, columns, lines).transpose(0, 2, 1)


def solution(mesh):
    in_specs = (
        P("owner", None, None),
        P("view", "owner", None, None),
        P("view", "owner", None, None),
        P("view", None, None),
        P("view", None, None),
        P("owner", None, None),
    )
    out_specs = P("owner", None, None)
    return jax.shard_map(local, mesh=mesh, in_specs=in_specs, out_specs=out_specs, check_vma=False)
```

```python
import functools

import jax
import jax.numpy as jnp
from jax import lax
from jax.experimental import pallas as pl
from jax.experimental.pallas import tpu as pltpu
from jax.sharding import PartitionSpec as P

ITERS = 2
VA = 4
RIM = 16
UNROLL = 4
BF = jnp.bfloat16
F32 = jnp.float32

COLS = 8
GROUPS = [list(range(8 * g, 8 * g + 8)) for g in range(4)]
Z_UP = [(8 * x + k, 8 * x + 8 + k) for x in range(3) for k in range(8)]
Z_DOWN = [(b, a) for a, b in Z_UP]
X_UP = [(8 * x + k, 8 * x + k + 1) for x in range(4) for k in range(7)]
X_DOWN = [(b, a) for a, b in X_UP]
V_UP = [(i, (i + 1) % 4) for i in range(4)]
V_DOWN = [(b, a) for a, b in V_UP]


def lateral_round(t):
    return [
        (4 * k + r, ((r + t + k // 2) % 4) * 8 + k) for k in range(8) for r in range(4)
    ]


def split(value):
    hi = value.astype(BF)
    lo = (value - hi.astype(F32)).astype(BF)
    return hi, lo


def band(kernel, length, extended):
    rim = RIM if extended else 0
    taps = kernel.shape[-1]
    row = jnp.arange(length)[:, None]
    col = jnp.arange(length + 2 * rim)[None, :]
    offset = col - row + (RIM - rim)
    hit = offset[:, :, None] == jnp.arange(taps)[None, None, :]
    return jnp.sum(jnp.where(hit, kernel[..., None, None, :], 0.0), axis=-1)


def edge_weights(kernel, positions, total):
    source = positions[:, None] + jnp.arange(kernel.shape[-1])[None, :] - RIM
    inside = (source >= 0) & (source < total)
    return jnp.sum(jnp.where(inside, kernel[..., None, :], 0.0), axis=-1)


def split_matrix(value):
    hi = lax.reduce_precision(value, 8, 7)
    return hi.astype(BF), (value - hi).astype(BF)


def left_form(matrix):
    hi, lo = split_matrix(matrix)
    return jnp.concatenate([hi, lo, hi], axis=-1)


def right_form(matrix):
    hi, lo = split_matrix(matrix)
    return jnp.concatenate([hi, lo, hi], axis=-2)


def dot(a, b):
    return lax.dot_general(a, b, (((1,), (0,)), ((), ())), preferred_element_type=F32)


def conv_rows(matrix, data):
    hi, lo = split(data)
    return dot(matrix, jnp.concatenate([hi, hi, lo], axis=0))


def conv_lanes(data, matrix):
    hi, lo = split(data)
    return dot(jnp.concatenate([hi, hi, lo], axis=1), matrix)


def xy_planes(load, mx, my, planes, mid_ref, finish):
    group = 2 * UNROLL
    steps = planes // group

    def along_x(i):
        for u in range(0, group, 2):
            p = group * i + u
            mid = conv_rows(mx, jnp.concatenate([load(p), load(p + 1)], axis=1))
            half = mid.shape[0]
            slot = lax.rem(i, 2)
            mid_ref[slot, u * half : (u + 1) * half] = mid[:, :128]
            mid_ref[slot, (u + 1) * half : (u + 2) * half] = mid[:, 128:]

    def along_y(i):
        done = conv_lanes(mid_ref[lax.rem(i, 2)], my)
        half = done.shape[0] // group
        for u in range(group):
            finish(group * i + u, done[u * half : (u + 1) * half])

    def body(i, _):
        along_y(i - 1)
        along_x(i)
        return 0

    along_x(0)
    lax.fori_loop(1, steps, body, 0)
    along_y(steps - 1)


def z_columns(load, mz, columns, store):
    def body(i, _):
        for u in range(UNROLL):
            x = 2 * (UNROLL * i + u)
            out = conv_rows(mz, jnp.concatenate([load(x), load(x + 1)], axis=1))
            store(x, out[:, :128])
            store(x + 1, out[:, 128:])
        return 0

    lax.fori_loop(0, columns // (2 * UNROLL), body, 0)


def each(count, step):
    def body(i, _):
        for u in range(UNROLL):
            step(UNROLL * i + u)
        return 0

    lax.fori_loop(0, count // UNROLL, body, 0)


def forward_kernel(
    mz_ref, mx_ref, my_ref, f_ref, zb_ref, za_ref, xl_ref, xr_ref, cl_ref, cr_ref, obs_ref,
    q_ref, first_ref, last_ref, e_ref, w_ref, mid_ref,
):
    depth, width = f_ref.shape[0], f_ref.shape[1]
    wide = width + 2 * RIM
    pitch = wide + 1
    part = width + 1
    mz = mz_ref[...]

    def middle(source, start):
        def step(z):
            e_ref[pl.ds((start + z) * pitch + RIM, width), :] = source[z]

        each(source.shape[0], step)

    def edge(z, left, right):
        e_ref[pl.ds(z * pitch, RIM), :] = left
        e_ref[pl.ds(z * pitch + RIM + width, RIM), :] = right

    def sides(z):
        edge(RIM + z, xl_ref[z], xr_ref[z])

    def corners(z):
        edge(z, cl_ref[z], cr_ref[z])
        edge(RIM + depth + z, cl_ref[RIM + z], cr_ref[RIM + z])

    middle(zb_ref, 0)
    middle(f_ref, RIM)
    middle(za_ref, RIM + depth)
    each(depth, sides)
    each(RIM, corners)

    def load(x):
        return e_ref[pl.ds(x, depth + 2 * RIM, stride=pitch), :]

    def store(x, value):
        w_ref[pl.ds(x, depth, stride=pitch), :] = value

    z_columns(load, mz, wide, store)

    def finish(p, blurred):
        q_ref[pl.ds(p * part, width), :] = obs_ref[p] / blurred

    xy_planes(
        lambda p: w_ref[pl.ds(p * pitch, wide), :], mx_ref[...], my_ref[...], depth, mid_ref, finish
    )

    def edges(z):
        first_ref[z] = q_ref[pl.ds(z * part, width), :]
        last_ref[z] = q_ref[pl.ds((depth - RIM + z) * part, width), :]

    each(RIM, edges)


def back_z_kernel(mz_ref, q_ref, zb_ref, za_ref, r_ref, first_ref, last_ref, b_ref, a_ref):
    width = zb_ref.shape[1]
    part = width + 1
    depth = q_ref.shape[0] // part

    def rims(z):
        b_ref[pl.ds(z * part, width), :] = zb_ref[z]
        a_ref[pl.ds(z * part, width), :] = za_ref[z]

    each(RIM, rims)

    def load(x):
        return jnp.concatenate(
            [
                b_ref[pl.ds(x, RIM, stride=part), :],
                q_ref[pl.ds(x, depth, stride=part), :],
                a_ref[pl.ds(x, RIM, stride=part), :],
            ],
            axis=0,
        )

    def store(x, value):
        r_ref[pl.ds(x, depth, stride=part), :] = value

    z_columns(load, mz_ref[...], width, store)

    def edges(z):
        first_ref[z] = r_ref[pl.ds(z * part, RIM), :]
        last_ref[z] = r_ref[pl.ds(z * part + width - RIM, RIM), :]

    each(depth, edges)


def back_xy_kernel(me_ref, w_ref, mx_ref, my_ref, r_ref, xl_ref, xr_ref, *rest):
    acc_ref, l_ref, mid_ref = rest if len(rest) == 3 else (None, *rest)
    me = me_ref[0]
    depth = xl_ref.shape[0]
    part = r_ref.shape[0] // depth

    def load(p):
        return jnp.concatenate(
            [xl_ref[p], r_ref[pl.ds(p * part, part - 1), :], xr_ref[p]], axis=0
        )

    def finish(p, back):
        term = w_ref[lax.div(p, 16)] * jnp.log(back)
        for quarter in range(4):
            slot = lax.rem(quarter - me + 4, 4)
            piece = term[quarter * 16 : quarter * 16 + 16]
            if acc_ref is not None:
                piece = piece + acc_ref[slot, p]
            l_ref[slot, p] = piece

    xy_planes(load, mx_ref[...], my_ref[...], depth, mid_ref, finish)


def assemble_kernel(at_ref, *refs):
    *pieces, block_ref, first_ref, last_ref, low_ref, high_ref = refs
    depth, narrow = pieces[0].shape[0], pieces[0].shape[1]
    for number, piece in enumerate(pieces):
        at = pl.multiple_of(at_ref[number], narrow)

        def step(z):
            block_ref[z, pl.ds(at, narrow), :] = piece[z]

        each(depth, step)
    first_ref[...] = block_ref[:RIM]
    last_ref[...] = block_ref[depth - RIM :]
    width = block_ref.shape[1]
    low_ref[...] = block_ref[:, :RIM]
    high_ref[...] = block_ref[:, width - RIM :]


VMEM = pl.BlockSpec(memory_space=pltpu.VMEM)
SMEM = pl.BlockSpec(memory_space=pltpu.SMEM)


def params(mebibytes):
    return pltpu.CompilerParams(vmem_limit_bytes=mebibytes * 2**20)


def forward(mz, mx, my, f, zb, za, xl, xr, cl, cr, obs):
    depth, width, lines = f.shape
    rim = jax.ShapeDtypeStruct((RIM, width, lines), F32)
    pitch = width + 2 * RIM + 1
    return pl.pallas_call(
        forward_kernel,
        in_specs=[VMEM] * 11,
        out_specs=[VMEM] * 3,
        out_shape=[jax.ShapeDtypeStruct((depth * (width + 1), lines), F32), rim, rim],
        scratch_shapes=[
            pltpu.VMEM(((depth + 2 * RIM) * pitch, lines), F32),
            pltpu.VMEM((depth * pitch, lines), F32),
            pltpu.VMEM((2, 2 * UNROLL * width, lines), F32),
        ],
        compiler_params=params(20),
        cost_estimate=pl.CostEstimate(flops=10**10, bytes_accessed=2 * 10**7, transcendentals=0),
        name="forward",
    )(mz, mx, my, f, zb, za, xl, xr, cl, cr, obs)


def back_z(mz, q, zb, za):
    width, lines = zb.shape[1:]
    depth = q.shape[0] // (width + 1)
    rim = jax.ShapeDtypeStruct((depth, RIM, lines), F32)
    padded = pltpu.VMEM((RIM * (width + 1), lines), F32)
    return pl.pallas_call(
        back_z_kernel,
        in_specs=[VMEM] * 4,
        out_specs=[VMEM] * 3,
        out_shape=[jax.ShapeDtypeStruct(q.shape, F32), rim, rim],
        scratch_shapes=[padded, padded],
        compiler_params=params(12),
        cost_estimate=pl.CostEstimate(flops=3 * 10**9, bytes_accessed=10**7, transcendentals=0),
        name="back_z",
    )(mz, q, zb, za)


def back_xy(me, weight, mx, my, r, xl, xr, acc=None):
    depth, _, lines = xl.shape
    width = r.shape[0] // depth - 1
    args = [me, weight, mx, my, r, xl, xr] + ([] if acc is None else [acc])
    return pl.pallas_call(
        back_xy_kernel,
        in_specs=[SMEM, SMEM] + [VMEM] * (len(args) - 2),
        out_specs=VMEM,
        out_shape=jax.ShapeDtypeStruct((4, depth, width // 4, lines), F32),
        scratch_shapes=[pltpu.VMEM((2, 2 * UNROLL * width, lines), F32)],
        compiler_params=params(12),
        cost_estimate=pl.CostEstimate(flops=5 * 10**9, bytes_accessed=10**7, transcendentals=10**6),
        name="back_xy",
    )(*args)


def assemble(at, pieces):
    depth, narrow, lines = pieces[0].shape
    width = narrow * len(pieces)
    rim = jax.ShapeDtypeStruct((RIM, width, lines), F32)
    side = jax.ShapeDtypeStruct((depth, RIM, lines), F32)
    return pl.pallas_call(
        assemble_kernel,
        in_specs=[SMEM] + [VMEM] * len(pieces),
        out_specs=[VMEM] * 5,
        out_shape=[jax.ShapeDtypeStruct((depth, width, lines), F32), rim, rim, side, side],
        compiler_params=params(16),
        cost_estimate=pl.CostEstimate(flops=10**6, bytes_accessed=10**7, transcendentals=0),
        name="assemble",
    )(at.astype(jnp.int32), *pieces)


def gather_quarters(quarter, half):
    below = lax.ppermute(quarter, "view", V_UP)
    above = lax.ppermute(quarter, "view", V_DOWN)
    first = lax.ppermute(below[:half], "view", V_UP)
    second = lax.ppermute(above[half:], "view", V_DOWN)
    return quarter, above, jnp.concatenate([first, second], axis=0), below


def scatter_quarters(parts):
    half = parts.shape[1] // 2
    first = lax.ppermute(parts[2, :half], "view", V_UP)
    second = lax.ppermute(parts[2, half:], "view", V_DOWN)
    up = jnp.concatenate([parts[1, :half] + first, parts[1, half:]], axis=0)
    down = jnp.concatenate([parts[3, :half], parts[3, half:] + second], axis=0)
    return parts[0] + lax.ppermute(up, "view", V_UP) + lax.ppermute(down, "view", V_DOWN)


def to_blocks(value):
    return lax.all_to_all(
        value, "owner", split_axis=1, concat_axis=0, axis_index_groups=GROUPS, tiled=True
    )


def z_rims(first, last):
    before = lax.ppermute(last, "owner", Z_UP)
    after = lax.ppermute(first, "owner", Z_DOWN)
    return before, after


def x_rims(first, last):
    left = lax.ppermute(last, "owner", X_UP)
    right = lax.ppermute(first, "owner", X_DOWN)
    return left, right


def local(estimate, axial_views, lateral_views, psf_axial, psf_lateral, coverage):
    slab, lines, columns = estimate.shape
    owner = lax.axis_index("owner")
    me = lax.axis_index("view")
    k = owner % 8
    z_chip = owner // 8
    width = columns // COLS
    depth = 8 * slab

    turned = estimate.transpose(0, 2, 1).reshape(slab, COLS, 4, width // 4, lines)
    mine = lax.dynamic_index_in_dim(turned, me, 2, keepdims=False)
    cover = jnp.repeat(coverage[0].astype(F32), 2, axis=0)
    cover = jnp.pad(cover[:, None, :], ((0, 0), (0, width // 4 - 1), (0, lines - cover.shape[1])))
    mine = jnp.concatenate([mine, cover[None]], axis=0).reshape(slab + 1, -1, lines)
    lateral_views, mine = lax.optimization_barrier((lateral_views, mine))
    got = to_blocks(mine).reshape(8, slab + 1, width // 4, lines)
    quarter = got[:, :slab].reshape(depth, width // 4, lines)
    cover = got[:, slab, 0, :8]

    chunks = lateral_views[0].transpose(2, 0, 1).reshape(4, depth, slab, lines)
    pieces, places = [], []
    for t in range(4):
        target = (owner % 4 + t + z_chip) % 4
        pieces.append(lax.dynamic_index_in_dim(chunks, target, 0, keepdims=False))
        places.append(((z_chip - t - k // 2) % 4) * slab)
    axial_views, *pieces = lax.optimization_barrier((axial_views, *pieces))
    pieces = [lax.ppermute(piece, "owner", lateral_round(t)) for t, piece in enumerate(pieces)]
    axial = to_blocks(axial_views[0].transpose(0, 2, 1))
    lateral = assemble(jnp.stack(places), pieces)[0]

    count = jnp.sum(cover, axis=-1)
    weight_axial = lax.dynamic_index_in_dim(cover, me, 1, keepdims=False)
    weight_lateral = lax.dynamic_index_in_dim(cover, VA + me, 1, keepdims=False)

    taps = jnp.concatenate([psf_axial, psf_lateral], axis=0)
    taps = taps / jnp.sum(taps, axis=-1, keepdims=True)
    flipped = taps[..., ::-1]
    z_at = z_chip * depth + jnp.arange(depth)
    x_at = k * width + jnp.arange(width)
    y_at = jnp.arange(lines)
    ahead_z = left_form(band(taps[:, 0], depth, True))
    ahead_x = left_form(band(taps[:, 2], width, True))
    ahead_y = right_form(jnp.swapaxes(band(taps[:, 1], lines, False), 1, 2))
    wz = edge_weights(flipped[:, 0], z_at, 4 * depth)
    wx = edge_weights(flipped[:, 2], x_at, columns)
    wy = edge_weights(flipped[:, 1], y_at, lines)
    back_mz = left_form(band(flipped[:, 0], depth, True) / wz[:, :, None])
    back_mx = left_form(band(flipped[:, 2], width, True) / wx[:, :, None])
    back_my = right_form(
        jnp.swapaxes(band(flipped[:, 1], lines, False) / wy[:, :, None], 1, 2)
    )
    me_arr = me[None].astype(jnp.int32)

    for iteration in range(ITERS):
        pieces = gather_quarters(quarter, depth // 2)
        places = ((me + jnp.arange(4)) % 4) * (width // 4)
        block, first, last, low, high = assemble(places, pieces)
        before, after = z_rims(first, last)
        left, right = x_rims(low, high)
        corner_left, corner_right = x_rims(
            jnp.concatenate([before[:, :RIM], after[:, :RIM]], axis=0),
            jnp.concatenate([before[:, -RIM:], after[:, -RIM:]], axis=0),
        )
        logs = None
        for number, (obs, weight) in enumerate(
            ((axial, weight_axial), (lateral, weight_lateral))
        ):
            quotient, first, last = forward(
                ahead_z[number], ahead_x[number], ahead_y[number],
                block, before, after, left, right, corner_left, corner_right, obs,
            )
            rz, low, high = back_z(back_mz[number], quotient, *z_rims(first, last))
            logs = back_xy(
                me_arr, weight, back_mx[number], back_my[number],
                rz, *x_rims(low, high), acc=logs,
            )
        total = scatter_quarters(logs)
        slabs = total.reshape(8, slab, width // 4, lines) / count[:, None, None, None]
        quarter = quarter * jnp.exp(slabs.reshape(quarter.shape))

    slabs = lax.all_to_all(
        quarter, "owner", split_axis=0, concat_axis=1, axis_index_groups=GROUPS, tiled=True
    )
    pieces = gather_quarters(slabs, slab // 2)
    pieces = [piece.reshape(slab * COLS, width // 4, lines) for piece in pieces]
    result = assemble(((me + jnp.arange(4)) % 4) * (width // 4), pieces)[0]
    return result.reshape(slab, columns, lines).transpose(0, 2, 1)


def solution(mesh):
    in_specs = (
        P("owner", None, None),
        P("view", "owner", None, None),
        P("view", "owner", None, None),
        P("view", None, None),
        P("view", None, None),
        P("owner", None, None),
    )
    out_specs = P("owner", None, None)
    return jax.shard_map(local, mesh=mesh, in_specs=in_specs, out_specs=out_specs, check_vma=False)
```

```python
import functools

import jax
import jax.numpy as jnp
from jax import lax
from jax.experimental import pallas as pl
from jax.experimental.pallas import tpu as pltpu
from jax.sharding import PartitionSpec as P

ITERS = 2
VA = 4
RIM = 16
UNROLL = 4
BF = jnp.bfloat16
F32 = jnp.float32

COLS = 8
GROUPS = [list(range(8 * g, 8 * g + 8)) for g in range(4)]
Z_UP = [(8 * x + k, 8 * x + 8 + k) for x in range(3) for k in range(8)]
Z_DOWN = [(b, a) for a, b in Z_UP]
X_UP = [(8 * x + k, 8 * x + k + 1) for x in range(4) for k in range(7)]
X_DOWN = [(b, a) for a, b in X_UP]
V_UP = [(i, (i + 1) % 4) for i in range(4)]
V_DOWN = [(b, a) for a, b in V_UP]


def diagonal(dz, dx):
    return [
        (8 * x + k, 8 * (x + dz) + k + dx)
        for x in range(4)
        for k in range(8)
        if 0 <= x + dz < 4 and 0 <= k + dx < 8
    ]


def lateral_round(t):
    return [
        (4 * k + r, ((r + t + k // 2) % 4) * 8 + k) for k in range(8) for r in range(4)
    ]


def split(value):
    hi = value.astype(BF)
    lo = (value - hi.astype(F32)).astype(BF)
    return hi, lo


def band(kernel, length, extended):
    rim = RIM if extended else 0
    taps = kernel.shape[-1]
    row = jnp.arange(length)[:, None]
    col = jnp.arange(length + 2 * rim)[None, :]
    offset = col - row + (RIM - rim)
    hit = offset[:, :, None] == jnp.arange(taps)[None, None, :]
    return jnp.sum(jnp.where(hit, kernel[..., None, None, :], 0.0), axis=-1)


def edge_weights(kernel, positions, total):
    source = positions[:, None] + jnp.arange(kernel.shape[-1])[None, :] - RIM
    inside = (source >= 0) & (source < total)
    return jnp.sum(jnp.where(inside, kernel[..., None, :], 0.0), axis=-1)


def split_matrix(value):
    hi = lax.reduce_precision(value, 8, 7)
    return hi.astype(BF), (value - hi).astype(BF)


def left_form(matrix):
    hi, lo = split_matrix(matrix)
    return jnp.concatenate([hi, lo, hi], axis=-1)


def right_form(matrix):
    hi, lo = split_matrix(matrix)
    top = jnp.concatenate([hi, lo], axis=-1)
    low = jnp.concatenate([hi, jnp.zeros_like(lo)], axis=-1)
    return jnp.concatenate([top, low], axis=-2)


def dot(a, b):
    return lax.dot_general(a, b, (((1,), (0,)), ((), ())), preferred_element_type=F32)


def conv_rows(matrix, data):
    hi, lo = split(data)
    return dot(matrix, jnp.concatenate([hi, hi, lo], axis=0))


def conv_lanes(data, matrix):
    hi, lo = split(data)
    both = dot(jnp.concatenate([hi, lo], axis=1), matrix)
    half = data.shape[1]
    return both[:, :half] + both[:, half:]


def xy_planes(load, mx, my, planes, mid_ref, finish):
    group = 2 * UNROLL
    steps = planes // group

    def along_x(i):
        for u in range(0, group, 2):
            p = group * i + u
            mid = conv_rows(mx, jnp.concatenate([load(p), load(p + 1)], axis=1))
            half = mid.shape[0]
            slot = lax.rem(i, 2)
            mid_ref[slot, u * half : (u + 1) * half] = mid[:, :128]
            mid_ref[slot, (u + 1) * half : (u + 2) * half] = mid[:, 128:]

    def along_y(i):
        done = conv_lanes(mid_ref[lax.rem(i, 2)], my)
        half = done.shape[0] // group
        for u in range(group):
            finish(group * i + u, done[u * half : (u + 1) * half])

    def body(i, _):
        along_y(i - 1)
        along_x(i)
        return 0

    along_x(0)
    lax.fori_loop(1, steps, body, 0)
    along_y(steps - 1)


def z_columns(load, mz, columns, store):
    def body(i, _):
        for u in range(UNROLL):
            x = 2 * (UNROLL * i + u)
            out = conv_rows(mz, jnp.concatenate([load(x), load(x + 1)], axis=1))
            store(x, out[:, :128])
            store(x + 1, out[:, 128:])
        return 0

    lax.fori_loop(0, columns // (2 * UNROLL), body, 0)


def each(count, step):
    def body(i, _):
        for u in range(UNROLL):
            step(UNROLL * i + u)
        return 0

    lax.fori_loop(0, count // UNROLL, body, 0)


def forward_kernel(
    mz_ref, mx_ref, my_ref, f_ref, zb_ref, za_ref, xl_ref, xr_ref, cl_ref, cr_ref, obs_ref,
    q_ref, first_ref, last_ref, e_ref, w_ref, mid_ref,
):
    depth, width = f_ref.shape[0], f_ref.shape[1]
    wide = width + 2 * RIM
    pitch = wide + 1
    part = width + 1
    mz = mz_ref[...]

    def middle(source, start):
        def step(z):
            e_ref[pl.ds((start + z) * pitch + RIM, width), :] = source[z]

        each(source.shape[0], step)

    def edge(z, left, right):
        e_ref[pl.ds(z * pitch, RIM), :] = left
        e_ref[pl.ds(z * pitch + RIM + width, RIM), :] = right

    def sides(z):
        edge(RIM + z, xl_ref[z], xr_ref[z])

    def corners(z):
        edge(z, cl_ref[z], cr_ref[z])
        edge(RIM + depth + z, cl_ref[RIM + z], cr_ref[RIM + z])

    middle(zb_ref, 0)
    middle(f_ref, RIM)
    middle(za_ref, RIM + depth)
    each(depth, sides)
    each(RIM, corners)

    def load(x):
        return e_ref[pl.ds(x, depth + 2 * RIM, stride=pitch), :]

    def store(x, value):
        w_ref[pl.ds(x, depth, stride=pitch), :] = value

    z_columns(load, mz, wide, store)

    def finish(p, blurred):
        q_ref[pl.ds(p * part, width), :] = obs_ref[p] / blurred

    xy_planes(
        lambda p: w_ref[pl.ds(p * pitch, wide), :], mx_ref[...], my_ref[...], depth, mid_ref, finish
    )

    def edges(z):
        first_ref[z] = q_ref[pl.ds(z * part, width), :]
        last_ref[z] = q_ref[pl.ds((depth - RIM + z) * part, width), :]

    each(RIM, edges)


def back_z_kernel(mz_ref, q_ref, zb_ref, za_ref, r_ref, first_ref, last_ref, b_ref, a_ref):
    width = zb_ref.shape[1]
    part = width + 1
    depth = q_ref.shape[0] // part

    def rims(z):
        b_ref[pl.ds(z * part, width), :] = zb_ref[z]
        a_ref[pl.ds(z * part, width), :] = za_ref[z]

    each(RIM, rims)

    def load(x):
        return jnp.concatenate(
            [
                b_ref[pl.ds(x, RIM, stride=part), :],
                q_ref[pl.ds(x, depth, stride=part), :],
                a_ref[pl.ds(x, RIM, stride=part), :],
            ],
            axis=0,
        )

    def store(x, value):
        r_ref[pl.ds(x, depth, stride=part), :] = value

    z_columns(load, mz_ref[...], width, store)

    def edges(z):
        first_ref[z] = r_ref[pl.ds(z * part, RIM), :]
        last_ref[z] = r_ref[pl.ds(z * part + width - RIM, RIM), :]

    each(depth, edges)


def back_xy_kernel(me_ref, w_ref, mx_ref, my_ref, r_ref, xl_ref, xr_ref, *rest):
    acc_ref, l_ref, mid_ref = rest if len(rest) == 3 else (None, *rest)
    me = me_ref[0]
    depth = xl_ref.shape[0]
    part = r_ref.shape[0] // depth

    def load(p):
        return jnp.concatenate(
            [xl_ref[p], r_ref[pl.ds(p * part, part - 1), :], xr_ref[p]], axis=0
        )

    def finish(p, back):
        term = w_ref[lax.div(p, 16)] * jnp.log(back)
        for quarter in range(4):
            slot = lax.rem(quarter - me + 4, 4)
            piece = term[quarter * 16 : quarter * 16 + 16]
            if acc_ref is not None:
                piece = piece + acc_ref[slot, p]
            l_ref[slot, p] = piece

    xy_planes(load, mx_ref[...], my_ref[...], depth, mid_ref, finish)


def assemble_kernel(at_ref, *refs):
    *pieces, block_ref, first_ref, last_ref, low_ref, high_ref = refs
    depth, narrow = pieces[0].shape[0], pieces[0].shape[1]
    for number, piece in enumerate(pieces):
        at = pl.multiple_of(at_ref[number], narrow)

        def step(z):
            block_ref[z, pl.ds(at, narrow), :] = piece[z]

        each(depth, step)
    first_ref[...] = block_ref[:RIM]
    last_ref[...] = block_ref[depth - RIM :]
    width = block_ref.shape[1]
    low_ref[...] = block_ref[:, :RIM]
    high_ref[...] = block_ref[:, width - RIM :]


def turn_kernel(at_ref, *refs):
    *pieces, out_ref, rows_ref = refs
    slab, columns = out_ref.shape[0], out_ref.shape[2]
    narrow = pieces[0].shape[1]
    width = narrow * len(pieces)
    count = columns // width
    starts = [pl.multiple_of(at_ref[number], narrow) for number in range(len(pieces))]

    def step(z, _):
        for number, piece in enumerate(pieces):
            for g in range(count):
                rows_ref[pl.ds(g * width + starts[number], narrow), :] = piece[z * count + g]
        out_ref[z] = rows_ref[...].T
        return 0

    lax.fori_loop(0, slab, step, 0)


VMEM = pl.BlockSpec(memory_space=pltpu.VMEM)
SMEM = pl.BlockSpec(memory_space=pltpu.SMEM)


def params(mebibytes):
    return pltpu.CompilerParams(vmem_limit_bytes=mebibytes * 2**20)


def forward(mz, mx, my, f, zb, za, xl, xr, cl, cr, obs):
    depth, width, lines = f.shape
    rim = jax.ShapeDtypeStruct((RIM, width, lines), F32)
    pitch = width + 2 * RIM + 1
    return pl.pallas_call(
        forward_kernel,
        in_specs=[VMEM] * 11,
        out_specs=[VMEM] * 3,
        out_shape=[jax.ShapeDtypeStruct((depth * (width + 1), lines), F32), rim, rim],
        scratch_shapes=[
            pltpu.VMEM(((depth + 2 * RIM) * pitch, lines), F32),
            pltpu.VMEM((depth * pitch, lines), F32),
            pltpu.VMEM((2, 2 * UNROLL * width, lines), F32),
        ],
        compiler_params=params(20),
        cost_estimate=pl.CostEstimate(flops=10**10, bytes_accessed=2 * 10**7, transcendentals=0),
        name="forward",
    )(mz, mx, my, f, zb, za, xl, xr, cl, cr, obs)


def back_z(mz, q, zb, za):
    width, lines = zb.shape[1:]
    depth = q.shape[0] // (width + 1)
    rim = jax.ShapeDtypeStruct((depth, RIM, lines), F32)
    padded = pltpu.VMEM((RIM * (width + 1), lines), F32)
    return pl.pallas_call(
        back_z_kernel,
        in_specs=[VMEM] * 4,
        out_specs=[VMEM] * 3,
        out_shape=[jax.ShapeDtypeStruct(q.shape, F32), rim, rim],
        scratch_shapes=[padded, padded],
        compiler_params=params(12),
        cost_estimate=pl.CostEstimate(flops=3 * 10**9, bytes_accessed=10**7, transcendentals=0),
        name="back_z",
    )(mz, q, zb, za)


def back_xy(me, weight, mx, my, r, xl, xr, acc=None):
    depth, _, lines = xl.shape
    width = r.shape[0] // depth - 1
    args = [me, weight, mx, my, r, xl, xr] + ([] if acc is None else [acc])
    return pl.pallas_call(
        back_xy_kernel,
        in_specs=[SMEM, SMEM] + [VMEM] * (len(args) - 2),
        out_specs=VMEM,
        out_shape=jax.ShapeDtypeStruct((4, depth, width // 4, lines), F32),
        scratch_shapes=[pltpu.VMEM((2, 2 * UNROLL * width, lines), F32)],
        compiler_params=params(12),
        cost_estimate=pl.CostEstimate(flops=5 * 10**9, bytes_accessed=10**7, transcendentals=10**6),
        name="back_xy",
    )(*args)


def assemble(at, pieces):
    depth, narrow, lines = pieces[0].shape
    width = narrow * len(pieces)
    rim = jax.ShapeDtypeStruct((RIM, width, lines), F32)
    side = jax.ShapeDtypeStruct((depth, RIM, lines), F32)
    return pl.pallas_call(
        assemble_kernel,
        in_specs=[SMEM] + [VMEM] * len(pieces),
        out_specs=[VMEM] * 5,
        out_shape=[jax.ShapeDtypeStruct((depth, width, lines), F32), rim, rim, side, side],
        compiler_params=params(16),
        cost_estimate=pl.CostEstimate(flops=10**6, bytes_accessed=10**7, transcendentals=0),
        name="assemble",
    )(at.astype(jnp.int32), *pieces)


def turn(at, pieces, slab):
    rows, narrow, lines = pieces[0].shape
    columns = rows // slab * narrow * len(pieces)
    return pl.pallas_call(
        turn_kernel,
        in_specs=[SMEM] + [VMEM] * len(pieces),
        out_specs=VMEM,
        out_shape=jax.ShapeDtypeStruct((slab, lines, columns), F32),
        scratch_shapes=[pltpu.VMEM((columns, lines), F32)],
        compiler_params=params(16),
        name="turn",
    )(at.astype(jnp.int32), *pieces)


def gather_quarters(quarter, half):
    below = lax.ppermute(quarter, "view", V_UP)
    above = lax.ppermute(quarter, "view", V_DOWN)
    first = lax.ppermute(below[:half], "view", V_UP)
    second = lax.ppermute(above[half:], "view", V_DOWN)
    return quarter, above, jnp.concatenate([first, second], axis=0), below


def scatter_quarters(parts):
    half = parts.shape[1] // 2
    first = lax.ppermute(parts[2, :half], "view", V_UP)
    second = lax.ppermute(parts[2, half:], "view", V_DOWN)
    up = jnp.concatenate([parts[1, :half] + first, parts[1, half:]], axis=0)
    down = jnp.concatenate([parts[3, :half], parts[3, half:] + second], axis=0)
    return parts[0] + lax.ppermute(up, "view", V_UP) + lax.ppermute(down, "view", V_DOWN)


def to_blocks(value):
    return lax.all_to_all(
        value, "owner", split_axis=1, concat_axis=0, axis_index_groups=GROUPS, tiled=True
    )


def z_rims(first, last):
    before = lax.ppermute(last, "owner", Z_UP)
    after = lax.ppermute(first, "owner", Z_DOWN)
    return before, after


def x_rims(first, last):
    left = lax.ppermute(last, "owner", X_UP)
    right = lax.ppermute(first, "owner", X_DOWN)
    return left, right


def local(estimate, axial_views, lateral_views, psf_axial, psf_lateral, coverage):
    slab, lines, columns = estimate.shape
    owner = lax.axis_index("owner")
    me = lax.axis_index("view")
    k = owner % 8
    z_chip = owner // 8
    width = columns // COLS
    depth = 8 * slab

    turned = estimate.transpose(0, 2, 1).reshape(slab, COLS, 4, width // 4, lines)
    mine = lax.dynamic_index_in_dim(turned, me, 2, keepdims=False)
    cover = jnp.repeat(coverage[0].astype(F32), 2, axis=0)
    cover = jnp.pad(cover[:, None, :], ((0, 0), (0, width // 4 - 1), (0, lines - cover.shape[1])))
    mine = jnp.concatenate([mine, cover[None]], axis=0).reshape(slab + 1, -1, lines)
    lateral_views, mine = lax.optimization_barrier((lateral_views, mine))
    got = to_blocks(mine).reshape(8, slab + 1, width // 4, lines)
    quarter = got[:, :slab].reshape(depth, width // 4, lines)
    cover = got[:, slab, 0, :8]

    chunks = lateral_views[0].transpose(2, 0, 1).reshape(4, depth, slab, lines)
    pieces, places = [], []
    for t in range(4):
        target = (owner % 4 + t + z_chip) % 4
        pieces.append(lax.dynamic_index_in_dim(chunks, target, 0, keepdims=False))
        places.append(((z_chip - t - k // 2) % 4) * slab)
    axial_views, *pieces = lax.optimization_barrier((axial_views, *pieces))
    pieces = [lax.ppermute(piece, "owner", lateral_round(t)) for t, piece in enumerate(pieces)]
    gathered = gather_quarters(quarter, depth // 2)
    axial_turned, *gathered = lax.optimization_barrier(
        (axial_views[0].transpose(0, 2, 1), *gathered)
    )
    axial = to_blocks(axial_turned)
    lateral = assemble(jnp.stack(places), pieces)[0]

    count = jnp.sum(cover, axis=-1)
    weight_axial = lax.dynamic_index_in_dim(cover, me, 1, keepdims=False)
    weight_lateral = lax.dynamic_index_in_dim(cover, VA + me, 1, keepdims=False)

    taps = jnp.concatenate([psf_axial, psf_lateral], axis=0)
    taps = taps / jnp.sum(taps, axis=-1, keepdims=True)
    flipped = taps[..., ::-1]
    z_at = z_chip * depth + jnp.arange(depth)
    x_at = k * width + jnp.arange(width)
    y_at = jnp.arange(lines)
    ahead_z = left_form(band(taps[:, 0], depth, True))
    ahead_x = left_form(band(taps[:, 2], width, True))
    ahead_y = right_form(jnp.swapaxes(band(taps[:, 1], lines, False), 1, 2))
    wz = edge_weights(flipped[:, 0], z_at, 4 * depth)
    wx = edge_weights(flipped[:, 2], x_at, columns)
    wy = edge_weights(flipped[:, 1], y_at, lines)
    back_mz = left_form(band(flipped[:, 0], depth, True) / wz[:, :, None])
    back_mx = left_form(band(flipped[:, 2], width, True) / wx[:, :, None])
    back_my = right_form(
        jnp.swapaxes(band(flipped[:, 1], lines, False) / wy[:, :, None], 1, 2)
    )
    me_arr = me[None].astype(jnp.int32)

    for iteration in range(ITERS):
        pieces = gather_quarters(quarter, depth // 2) if iteration else gathered
        places = ((me + jnp.arange(4)) % 4) * (width // 4)
        block, first, last, low, high = assemble(places, pieces)
        before, after = z_rims(first, last)
        left, right = x_rims(low, high)
        corner_left = jnp.concatenate(
            [
                lax.ppermute(last[:, -RIM:], "owner", diagonal(1, 1)),
                lax.ppermute(first[:, -RIM:], "owner", diagonal(-1, 1)),
            ],
            axis=0,
        )
        corner_right = jnp.concatenate(
            [
                lax.ppermute(last[:, :RIM], "owner", diagonal(1, -1)),
                lax.ppermute(first[:, :RIM], "owner", diagonal(-1, -1)),
            ],
            axis=0,
        )
        logs = None
        for number, (obs, weight) in [*enumerate(
            ((axial, weight_axial), (lateral, weight_lateral))
        )][::-1]:
            quotient, first, last = forward(
                ahead_z[number], ahead_x[number], ahead_y[number],
                block, before, after, left, right, corner_left, corner_right, obs,
            )
            rz, low, high = back_z(back_mz[number], quotient, *z_rims(first, last))
            logs = back_xy(
                me_arr, weight, back_mx[number], back_my[number],
                rz, *x_rims(low, high), acc=logs,
            )
        total = scatter_quarters(logs)
        slabs = total.reshape(8, slab, width // 4, lines) / count[:, None, None, None]
        quarter = quarter * jnp.exp(slabs.reshape(quarter.shape))

    slabs = lax.all_to_all(
        quarter, "owner", split_axis=0, concat_axis=1, axis_index_groups=GROUPS, tiled=True
    )
    pieces = gather_quarters(slabs, slab // 2)
    pieces = [piece.reshape(slab * COLS, width // 4, lines) for piece in pieces]
    return turn(((me + jnp.arange(4)) % 4) * (width // 4), pieces, slab)


def solution(mesh):
    in_specs = (
        P("owner", None, None),
        P("view", "owner", None, None),
        P("view", "owner", None, None),
        P("view", None, None),
        P("view", None, None),
        P("owner", None, None),
    )
    out_specs = P("owner", None, None)
    return jax.shard_map(local, mesh=mesh, in_specs=in_specs, out_specs=out_specs, check_vma=False)
```

```python
import jax
import jax.numpy as jnp
from jax import lax
from jax.experimental import pallas as pl
from jax.experimental.pallas import tpu as pltpu
from jax.sharding import PartitionSpec as P


ITERS = 2
VA = 4
RIM = 16
UNROLL = 4
BF = jnp.bfloat16
F32 = jnp.float32

COLS = 8
GROUPS = [list(range(8 * g, 8 * g + 8)) for g in range(4)]
Z_UP = [(8 * x + k, 8 * x + 8 + k) for x in range(3) for k in range(8)]
Z_DOWN = [(b, a) for a, b in Z_UP]
X_UP = [(8 * x + k, 8 * x + k + 1) for x in range(4) for k in range(7)]
X_DOWN = [(b, a) for a, b in X_UP]
V_UP = [(i, (i + 1) % 4) for i in range(4)]
V_DOWN = [(b, a) for a, b in V_UP]


def axial_round(d):
    return [(8 * x + k, 8 * x + (k + d) % 8) for x in range(4) for k in range(8)]


def lateral_round(t):
    return [
        (4 * k + r, ((r + t + k // 2) % 4) * 8 + k) for k in range(8) for r in range(4)
    ]


def split(value):
    hi = value.astype(BF)
    lo = (value - hi.astype(F32)).astype(BF)
    return hi, lo


def band(kernel, length, extended):
    rim = RIM if extended else 0
    taps = kernel.shape[-1]
    row = jnp.arange(length)[:, None]
    col = jnp.arange(length + 2 * rim)[None, :]
    offset = col - row + (RIM - rim)
    hit = offset[:, :, None] == jnp.arange(taps)[None, None, :]
    return jnp.sum(jnp.where(hit, kernel[..., None, None, :], 0.0), axis=-1)


def edge_weights(kernel, positions, total):
    source = positions[:, None] + jnp.arange(kernel.shape[-1])[None, :] - RIM
    inside = (source >= 0) & (source < total)
    return jnp.sum(jnp.where(inside, kernel[..., None, :], 0.0), axis=-1)


def split_matrix(value):
    hi = lax.reduce_precision(value, 8, 7)
    return hi.astype(BF), (value - hi).astype(BF)


def left_form(matrix):
    hi, lo = split_matrix(matrix)
    return jnp.concatenate([hi, lo, hi], axis=-1)


def right_form(matrix):
    hi, lo = split_matrix(matrix)
    top = jnp.concatenate([hi, lo], axis=-1)
    low = jnp.concatenate([hi, jnp.zeros_like(lo)], axis=-1)
    return jnp.concatenate([top, low], axis=-2)


def dot(a, b):
    return lax.dot_general(a, b, (((1,), (0,)), ((), ())), preferred_element_type=F32)


def conv_rows(matrix, data):
    hi, lo = split(data)
    return dot(matrix, jnp.concatenate([hi, hi, lo], axis=0))


def conv_lanes(data, matrix):
    hi, lo = split(data)
    both = dot(jnp.concatenate([hi, lo], axis=1), matrix)
    half = data.shape[1]
    return both[:, :half] + both[:, half:]


def xy_planes(load, mx, my, planes, mid_ref, finish):
    group = 2 * UNROLL
    steps = planes // group

    def along_x(i):
        for u in range(0, group, 2):
            p = group * i + u
            mid = conv_rows(mx, jnp.concatenate([load(p), load(p + 1)], axis=1))
            half = mid.shape[0]
            slot = lax.rem(i, 2)
            mid_ref[slot, u * half : (u + 1) * half] = mid[:, :128]
            mid_ref[slot, (u + 1) * half : (u + 2) * half] = mid[:, 128:]

    def along_y(i):
        done = conv_lanes(mid_ref[lax.rem(i, 2)], my)
        half = done.shape[0] // group
        for u in range(group):
            finish(group * i + u, done[u * half : (u + 1) * half])

    def body(i, _):
        along_y(i - 1)
        along_x(i)
        return 0

    along_x(0)
    lax.fori_loop(1, steps, body, 0)
    along_y(steps - 1)


def z_columns(load, mz, columns, store):
    def body(i, _):
        for u in range(UNROLL):
            x = 2 * (UNROLL * i + u)
            out = conv_rows(mz, jnp.concatenate([load(x), load(x + 1)], axis=1))
            store(x, out[:, :128])
            store(x + 1, out[:, 128:])
        return 0

    lax.fori_loop(0, columns // (2 * UNROLL), body, 0)


def each(count, step):
    def body(i, _):
        for u in range(UNROLL):
            step(UNROLL * i + u)
        return 0

    lax.fori_loop(0, count // UNROLL, body, 0)


def forward_kernel(
    mz_ref, mx_ref, my_ref, f_ref, zb_ref, za_ref, xl_ref, xr_ref, cl_ref, cr_ref, obs_ref,
    q_ref, first_ref, last_ref, e_ref, w_ref, mid_ref,
):
    depth, width = f_ref.shape[0], f_ref.shape[1]
    wide = width + 2 * RIM
    pitch = wide + 1
    part = width + 1
    mz = mz_ref[...]

    def middle(source, start):
        def step(z):
            e_ref[pl.ds((start + z) * pitch + RIM, width), :] = source[z]

        each(source.shape[0], step)

    def edge(z, left, right):
        e_ref[pl.ds(z * pitch, RIM), :] = left
        e_ref[pl.ds(z * pitch + RIM + width, RIM), :] = right

    def sides(z):
        edge(RIM + z, xl_ref[z], xr_ref[z])

    def corners(z):
        edge(z, cl_ref[z], cr_ref[z])
        edge(RIM + depth + z, cl_ref[RIM + z], cr_ref[RIM + z])

    middle(zb_ref, 0)
    middle(f_ref, RIM)
    middle(za_ref, RIM + depth)
    each(depth, sides)
    each(RIM, corners)

    def load(x):
        return e_ref[pl.ds(x, depth + 2 * RIM, stride=pitch), :]

    def store(x, value):
        w_ref[pl.ds(x, depth, stride=pitch), :] = value

    z_columns(load, mz, wide, store)

    def finish(p, blurred):
        q_ref[pl.ds(p * part, width), :] = obs_ref[p] / blurred

    xy_planes(
        lambda p: w_ref[pl.ds(p * pitch, wide), :], mx_ref[...], my_ref[...], depth, mid_ref, finish
    )

    def edges(z):
        first_ref[z] = q_ref[pl.ds(z * part, width), :]
        last_ref[z] = q_ref[pl.ds((depth - RIM + z) * part, width), :]

    each(RIM, edges)


def back_z_kernel(mz_ref, q_ref, zb_ref, za_ref, r_ref, first_ref, last_ref, b_ref, a_ref):
    width = zb_ref.shape[1]
    part = width + 1
    depth = q_ref.shape[0] // part

    def rims(z):
        b_ref[pl.ds(z * part, width), :] = zb_ref[z]
        a_ref[pl.ds(z * part, width), :] = za_ref[z]

    each(RIM, rims)

    def load(x):
        return jnp.concatenate(
            [
                b_ref[pl.ds(x, RIM, stride=part), :],
                q_ref[pl.ds(x, depth, stride=part), :],
                a_ref[pl.ds(x, RIM, stride=part), :],
            ],
            axis=0,
        )

    def store(x, value):
        r_ref[pl.ds(x, depth, stride=part), :] = value

    z_columns(load, mz_ref[...], width, store)

    def edges(z):
        first_ref[z] = r_ref[pl.ds(z * part, RIM), :]
        last_ref[z] = r_ref[pl.ds(z * part + width - RIM, RIM), :]

    each(depth, edges)


def back_xy_kernel(me_ref, w_ref, mx_ref, my_ref, r_ref, xl_ref, xr_ref, *rest):
    acc_ref, l_ref, mid_ref = rest if len(rest) == 3 else (None, *rest)
    me = me_ref[0]
    depth = xl_ref.shape[0]
    part = r_ref.shape[0] // depth

    def load(p):
        return jnp.concatenate(
            [xl_ref[p], r_ref[pl.ds(p * part, part - 1), :], xr_ref[p]], axis=0
        )

    def finish(p, back):
        term = w_ref[lax.div(p, 16)] * jnp.log(back)
        for quarter in range(4):
            slot = lax.rem(quarter - me + 4, 4)
            piece = term[quarter * 16 : quarter * 16 + 16]
            if acc_ref is not None:
                piece = piece + acc_ref[slot, p]
            l_ref[slot, p] = piece

    xy_planes(load, mx_ref[...], my_ref[...], depth, mid_ref, finish)


def assemble_kernel(at_ref, *refs):
    *pieces, block_ref, first_ref, last_ref, low_ref, high_ref = refs
    depth, narrow = pieces[0].shape[0], pieces[0].shape[1]
    for number, piece in enumerate(pieces):
        at = pl.multiple_of(at_ref[number], narrow)

        def step(z):
            block_ref[z, pl.ds(at, narrow), :] = piece[z]

        each(depth, step)
    first_ref[...] = block_ref[:RIM]
    last_ref[...] = block_ref[depth - RIM :]
    width = block_ref.shape[1]
    low_ref[...] = block_ref[:, :RIM]
    high_ref[...] = block_ref[:, width - RIM :]


def stack_kernel(at_ref, *refs):
    *pieces, block_ref = refs
    for number, piece in enumerate(pieces):
        block_ref[pl.ds(at_ref[number], piece.shape[0])] = piece[...]


def turn_kernel(at_ref, *refs):
    *pieces, out_ref, rows_ref = refs
    slab, columns = out_ref.shape[0], out_ref.shape[2]
    narrow = pieces[0].shape[1]
    width = narrow * len(pieces)
    count = columns // width
    starts = [pl.multiple_of(at_ref[number], narrow) for number in range(len(pieces))]

    def step(z, _):
        for number, piece in enumerate(pieces):
            for g in range(count):
                rows_ref[pl.ds(g * width + starts[number], narrow), :] = piece[z * count + g]
        out_ref[z] = rows_ref[...].T
        return 0

    lax.fori_loop(0, slab, step, 0)


VMEM = pl.BlockSpec(memory_space=pltpu.VMEM)
SMEM = pl.BlockSpec(memory_space=pltpu.SMEM)


def params(mebibytes):
    return pltpu.CompilerParams(vmem_limit_bytes=mebibytes * 2**20)


def forward(mz, mx, my, f, zb, za, xl, xr, cl, cr, obs):
    depth, width, lines = f.shape
    rim = jax.ShapeDtypeStruct((RIM, width, lines), F32)
    pitch = width + 2 * RIM + 1
    return pl.pallas_call(
        forward_kernel,
        in_specs=[VMEM] * 11,
        out_specs=[VMEM] * 3,
        out_shape=[jax.ShapeDtypeStruct((depth * (width + 1), lines), F32), rim, rim],
        scratch_shapes=[
            pltpu.VMEM(((depth + 2 * RIM) * pitch, lines), F32),
            pltpu.VMEM((depth * pitch, lines), F32),
            pltpu.VMEM((2, 2 * UNROLL * width, lines), F32),
        ],
        compiler_params=params(20),
        cost_estimate=pl.CostEstimate(flops=10**10, bytes_accessed=2 * 10**7, transcendentals=0),
        name="forward",
    )(mz, mx, my, f, zb, za, xl, xr, cl, cr, obs)


def back_z(mz, q, zb, za):
    width, lines = zb.shape[1:]
    depth = q.shape[0] // (width + 1)
    rim = jax.ShapeDtypeStruct((depth, RIM, lines), F32)
    padded = pltpu.VMEM((RIM * (width + 1), lines), F32)
    return pl.pallas_call(
        back_z_kernel,
        in_specs=[VMEM] * 4,
        out_specs=[VMEM] * 3,
        out_shape=[jax.ShapeDtypeStruct(q.shape, F32), rim, rim],
        scratch_shapes=[padded, padded],
        compiler_params=params(12),
        cost_estimate=pl.CostEstimate(flops=3 * 10**9, bytes_accessed=10**7, transcendentals=0),
        name="back_z",
    )(mz, q, zb, za)


def back_xy(me, weight, mx, my, r, xl, xr, acc=None):
    depth, _, lines = xl.shape
    width = r.shape[0] // depth - 1
    args = [me, weight, mx, my, r, xl, xr] + ([] if acc is None else [acc])
    return pl.pallas_call(
        back_xy_kernel,
        in_specs=[SMEM, SMEM] + [VMEM] * (len(args) - 2),
        out_specs=VMEM,
        out_shape=jax.ShapeDtypeStruct((4, depth, width // 4, lines), F32),
        scratch_shapes=[pltpu.VMEM((2, 2 * UNROLL * width, lines), F32)],
        compiler_params=params(12),
        cost_estimate=pl.CostEstimate(flops=5 * 10**9, bytes_accessed=10**7, transcendentals=10**6),
        name="back_xy",
    )(*args)


def assemble(at, pieces):
    depth, narrow, lines = pieces[0].shape
    width = narrow * len(pieces)
    rim = jax.ShapeDtypeStruct((RIM, width, lines), F32)
    side = jax.ShapeDtypeStruct((depth, RIM, lines), F32)
    return pl.pallas_call(
        assemble_kernel,
        in_specs=[SMEM] + [VMEM] * len(pieces),
        out_specs=[VMEM] * 5,
        out_shape=[jax.ShapeDtypeStruct((depth, width, lines), F32), rim, rim, side, side],
        compiler_params=params(16),
        cost_estimate=pl.CostEstimate(flops=10**6, bytes_accessed=10**7, transcendentals=0),
        name="assemble",
    )(at.astype(jnp.int32), *pieces)


def stack(at, pieces):
    slab, width, lines = pieces[0].shape
    return pl.pallas_call(
        stack_kernel,
        in_specs=[SMEM] + [VMEM] * len(pieces),
        out_specs=VMEM,
        out_shape=jax.ShapeDtypeStruct((slab * len(pieces), width, lines), F32),
        compiler_params=params(16),
        cost_estimate=pl.CostEstimate(flops=10**6, bytes_accessed=10**7, transcendentals=0),
        name="stack",
    )(at.astype(jnp.int32), *pieces)


def turn(at, pieces, slab):
    rows, narrow, lines = pieces[0].shape
    columns = rows // slab * narrow * len(pieces)
    return pl.pallas_call(
        turn_kernel,
        in_specs=[SMEM] + [VMEM] * len(pieces),
        out_specs=VMEM,
        out_shape=jax.ShapeDtypeStruct((slab, lines, columns), F32),
        scratch_shapes=[pltpu.VMEM((columns, lines), F32)],
        compiler_params=params(16),
        name="turn",
    )(at.astype(jnp.int32), *pieces)


def gather_quarters(quarter, half):
    below = lax.ppermute(quarter, "view", V_UP)
    above = lax.ppermute(quarter, "view", V_DOWN)
    first = lax.ppermute(below[:half], "view", V_UP)
    second = lax.ppermute(above[half:], "view", V_DOWN)
    return quarter, above, jnp.concatenate([first, second], axis=0), below


def scatter_quarters(parts):
    half = parts.shape[1] // 2
    first = lax.ppermute(parts[2, :half], "view", V_UP)
    second = lax.ppermute(parts[2, half:], "view", V_DOWN)
    up = jnp.concatenate([parts[1, :half] + first, parts[1, half:]], axis=0)
    down = jnp.concatenate([parts[3, :half], parts[3, half:] + second], axis=0)
    return parts[0] + lax.ppermute(up, "view", V_UP) + lax.ppermute(down, "view", V_DOWN)


def to_blocks(value):
    return lax.all_to_all(
        value, "owner", split_axis=1, concat_axis=0, axis_index_groups=GROUPS, tiled=True
    )


def z_rims(first, last):
    before = lax.ppermute(last, "owner", Z_UP)
    after = lax.ppermute(first, "owner", Z_DOWN)
    return before, after


def x_rims(first, last):
    left = lax.ppermute(last, "owner", X_UP)
    right = lax.ppermute(first, "owner", X_DOWN)
    return left, right


def local(estimate, axial_views, lateral_views, psf_axial, psf_lateral, coverage):
    slab, lines, columns = estimate.shape
    owner = lax.axis_index("owner")
    me = lax.axis_index("view")
    k = owner % 8
    z_chip = owner // 8
    width = columns // COLS
    depth = 8 * slab

    turned = estimate.transpose(0, 2, 1).reshape(slab, COLS, 4, width // 4, lines)
    mine = lax.dynamic_index_in_dim(turned, me, 2, keepdims=False)
    cover = jnp.repeat(coverage[0].astype(F32), 2, axis=0)
    cover = jnp.pad(cover[:, None, :], ((0, 0), (0, width // 4 - 1), (0, lines - cover.shape[1])))
    mine = jnp.concatenate([mine, cover[None]], axis=0).reshape(slab + 1, -1, lines)
    lateral_views, mine = lax.optimization_barrier((lateral_views, mine))
    got = to_blocks(mine).reshape(8, slab + 1, width // 4, lines)

    chunks = lateral_views[0].transpose(2, 0, 1).reshape(4, depth, slab, lines)
    pieces, places = [], []
    for t in range(4):
        target = (owner % 4 + t + z_chip) % 4
        pieces.append(lax.dynamic_index_in_dim(chunks, target, 0, keepdims=False))
        places.append(((z_chip - t - k // 2) % 4) * slab)
    axial_views, got, *pieces = lax.optimization_barrier((axial_views, got, *pieces))
    quarter = got[:, :slab].reshape(depth, width // 4, lines)
    cover = got[:, slab, 0, :8]
    pieces = [
        lax.ppermute(piece, "owner", lateral_round(t)) for t, piece in enumerate(pieces)
    ]
    axial_chunks = axial_views[0].transpose(0, 2, 1).reshape(slab, COLS, width, lines)
    axial_chunks = axial_chunks.transpose(1, 0, 2, 3)
    slabs = [
        lax.dynamic_index_in_dim(axial_chunks, (k + d) % 8, 0, keepdims=False) for d in range(8)
    ]
    slabs = [
        lax.ppermute(piece, "owner", axial_round(d)) if d else piece
        for d, piece in enumerate(slabs)
    ]
    axial = stack((k - jnp.arange(8)) % 8 * slab, slabs)
    lateral = assemble(jnp.stack(places), pieces)[0]

    count = jnp.sum(cover, axis=-1)
    weight_axial = lax.dynamic_index_in_dim(cover, me, 1, keepdims=False)
    weight_lateral = lax.dynamic_index_in_dim(cover, VA + me, 1, keepdims=False)

    taps = jnp.concatenate([psf_axial, psf_lateral], axis=0)
    taps = taps / jnp.sum(taps, axis=-1, keepdims=True)
    flipped = taps[..., ::-1]
    z_at = z_chip * depth + jnp.arange(depth)
    x_at = k * width + jnp.arange(width)
    y_at = jnp.arange(lines)
    ahead_z = left_form(band(taps[:, 0], depth, True))
    ahead_x = left_form(band(taps[:, 2], width, True))
    ahead_y = right_form(jnp.swapaxes(band(taps[:, 1], lines, False), 1, 2))
    wz = edge_weights(flipped[:, 0], z_at, 4 * depth)
    wx = edge_weights(flipped[:, 2], x_at, columns)
    wy = edge_weights(flipped[:, 1], y_at, lines)
    back_mz = left_form(band(flipped[:, 0], depth, True) / wz[:, :, None])
    back_mx = left_form(band(flipped[:, 2], width, True) / wx[:, :, None])
    back_my = right_form(
        jnp.swapaxes(band(flipped[:, 1], lines, False) / wy[:, :, None], 1, 2)
    )
    me_arr = me[None].astype(jnp.int32)

    for _ in range(ITERS):
        pieces = gather_quarters(quarter, depth // 2)
        places = ((me + jnp.arange(4)) % 4) * (width // 4)
        block, first, last, low, high = assemble(places, pieces)
        before, after = z_rims(first, last)
        left, right = x_rims(low, high)
        corner_left, corner_right = x_rims(
            jnp.concatenate([before[:, :RIM], after[:, :RIM]], axis=0),
            jnp.concatenate([before[:, -RIM:], after[:, -RIM:]], axis=0),
        )
        logs = None
        for number, (obs, weight) in [*enumerate(
            ((axial, weight_axial), (lateral, weight_lateral))
        )][::-1]:
            quotient, first, last = forward(
                ahead_z[number], ahead_x[number], ahead_y[number],
                block, before, after, left, right, corner_left, corner_right, obs,
            )
            rz, low, high = back_z(back_mz[number], quotient, *z_rims(first, last))
            logs = back_xy(
                me_arr, weight, back_mx[number], back_my[number],
                rz, *x_rims(low, high), acc=logs,
            )
        total = scatter_quarters(logs)
        slabs = total.reshape(8, slab, width // 4, lines) / count[:, None, None, None]
        quarter = quarter * jnp.exp(slabs.reshape(quarter.shape))

    slabs = lax.all_to_all(
        quarter, "owner", split_axis=0, concat_axis=1, axis_index_groups=GROUPS, tiled=True
    )
    pieces = gather_quarters(slabs, slab // 2)
    pieces = [piece.reshape(slab * COLS, width // 4, lines) for piece in pieces]
    return turn(((me + jnp.arange(4)) % 4) * (width // 4), pieces, slab)


def solution(mesh):
    in_specs = (
        P("owner", None, None),
        P("view", "owner", None, None),
        P("view", "owner", None, None),
        P("view", None, None),
        P("view", None, None),
        P("owner", None, None),
    )
    out_specs = P("owner", None, None)
    return jax.shard_map(local, mesh=mesh, in_specs=in_specs, out_specs=out_specs, check_vma=False)
```

```python
import jax
import jax.numpy as jnp
from jax import lax
from jax.experimental import pallas as pl
from jax.experimental.pallas import tpu as pltpu
from jax.sharding import PartitionSpec as P


ITERS = 2
VA = 4
RIM = 16
UNROLL = 4
BF = jnp.bfloat16
F32 = jnp.float32

COLS = 8
GROUPS = [list(range(8 * g, 8 * g + 8)) for g in range(4)]
Z_UP = [(8 * x + k, 8 * x + 8 + k) for x in range(3) for k in range(8)]
Z_DOWN = [(b, a) for a, b in Z_UP]
X_UP = [(8 * x + k, 8 * x + k + 1) for x in range(4) for k in range(7)]
X_DOWN = [(b, a) for a, b in X_UP]
V_UP = [(i, (i + 1) % 4) for i in range(4)]
V_DOWN = [(b, a) for a, b in V_UP]


def axial_round(d):
    return [(8 * x + k, 8 * x + (k + d) % 8) for x in range(4) for k in range(8)]


def lateral_round(t):
    return [
        (4 * k + r, ((r + t + k // 2) % 4) * 8 + k) for k in range(8) for r in range(4)
    ]


def split(value):
    hi = value.astype(BF)
    lo = (value - hi.astype(F32)).astype(BF)
    return hi, lo


def band(kernel, length, extended):
    rim = RIM if extended else 0
    taps = kernel.shape[-1]
    row = jnp.arange(length)[:, None]
    col = jnp.arange(length + 2 * rim)[None, :]
    offset = col - row + (RIM - rim)
    hit = offset[:, :, None] == jnp.arange(taps)[None, None, :]
    return jnp.sum(jnp.where(hit, kernel[..., None, None, :], 0.0), axis=-1)


def edge_weights(kernel, positions, total):
    source = positions[:, None] + jnp.arange(kernel.shape[-1])[None, :] - RIM
    inside = (source >= 0) & (source < total)
    return jnp.sum(jnp.where(inside, kernel[..., None, :], 0.0), axis=-1)


def split_matrix(value):
    hi = lax.reduce_precision(value, 8, 7)
    return hi.astype(BF), (value - hi).astype(BF)


def left_form(matrix):
    hi, lo = split_matrix(matrix)
    return jnp.concatenate([hi, lo, hi], axis=-1)


def right_form(matrix):
    hi, lo = split_matrix(matrix)
    top = jnp.concatenate([hi, lo], axis=-1)
    low = jnp.concatenate([hi, jnp.zeros_like(lo)], axis=-1)
    return jnp.concatenate([top, low], axis=-2)


def dot(a, b):
    return lax.dot_general(a, b, (((1,), (0,)), ((), ())), preferred_element_type=F32)


def conv_rows(matrix, data):
    hi, lo = split(data)
    return dot(matrix, jnp.concatenate([hi, hi, lo], axis=0))


def conv_lanes(data, matrix):
    hi, lo = split(data)
    both = dot(jnp.concatenate([hi, lo], axis=1), matrix)
    half = data.shape[1]
    return both[:, :half] + both[:, half:]


def xy_planes(load, mx, my, planes, mid_ref, finish):
    group = 2 * UNROLL
    steps = planes // group

    def along_x(i):
        for u in range(0, group, 2):
            p = group * i + u
            mid = conv_rows(mx, jnp.concatenate([load(p), load(p + 1)], axis=1))
            half = mid.shape[0]
            slot = lax.rem(i, 2)
            mid_ref[slot, u * half : (u + 1) * half] = mid[:, :128]
            mid_ref[slot, (u + 1) * half : (u + 2) * half] = mid[:, 128:]

    def along_y(i):
        done = conv_lanes(mid_ref[lax.rem(i, 2)], my)
        half = done.shape[0] // group
        for u in range(group):
            finish(group * i + u, done[u * half : (u + 1) * half])

    def body(i, _):
        along_y(i - 1)
        along_x(i)
        return 0

    along_x(0)
    lax.fori_loop(1, steps, body, 0)
    along_y(steps - 1)


def z_columns(load, mz, columns, store):
    def body(i, _):
        for u in range(UNROLL):
            x = 2 * (UNROLL * i + u)
            out = conv_rows(mz, jnp.concatenate([load(x), load(x + 1)], axis=1))
            store(x, out[:, :128])
            store(x + 1, out[:, 128:])
        return 0

    lax.fori_loop(0, columns // (2 * UNROLL), body, 0)


def each(count, step):
    def body(i, _):
        for u in range(UNROLL):
            step(UNROLL * i + u)
        return 0

    lax.fori_loop(0, count // UNROLL, body, 0)


def forward_kernel(
    mz_ref, mx_ref, my_ref, f_ref, zb_ref, za_ref, xl_ref, xr_ref, cl_ref, cr_ref, obs_ref,
    q_ref, first_ref, last_ref, e_ref, w_ref, mid_ref,
):
    depth, width = f_ref.shape[0], f_ref.shape[1]
    wide = width + 2 * RIM
    pitch = wide + 1
    part = width + 1
    mz = mz_ref[...]

    def middle(source, start):
        def step(z):
            e_ref[pl.ds((start + z) * pitch + RIM, width), :] = source[z]

        each(source.shape[0], step)

    def edge(z, left, right):
        e_ref[pl.ds(z * pitch, RIM), :] = left
        e_ref[pl.ds(z * pitch + RIM + width, RIM), :] = right

    def sides(z):
        edge(RIM + z, xl_ref[z], xr_ref[z])

    def corners(z):
        edge(z, cl_ref[z], cr_ref[z])
        edge(RIM + depth + z, cl_ref[RIM + z], cr_ref[RIM + z])

    middle(zb_ref, 0)
    middle(f_ref, RIM)
    middle(za_ref, RIM + depth)
    each(depth, sides)
    each(RIM, corners)

    def load(x):
        return e_ref[pl.ds(x, depth + 2 * RIM, stride=pitch), :]

    def store(x, value):
        w_ref[pl.ds(x, depth, stride=pitch), :] = value

    z_columns(load, mz, wide, store)

    def finish(p, blurred):
        q_ref[pl.ds(p * part, width), :] = obs_ref[p] / blurred

    xy_planes(
        lambda p: w_ref[pl.ds(p * pitch, wide), :], mx_ref[...], my_ref[...], depth, mid_ref, finish
    )

    def edges(z):
        first_ref[z] = q_ref[pl.ds(z * part, width), :]
        last_ref[z] = q_ref[pl.ds((depth - RIM + z) * part, width), :]

    each(RIM, edges)


def back_z_kernel(mz_ref, q_ref, zb_ref, za_ref, r_ref, first_ref, last_ref, b_ref, a_ref):
    width = zb_ref.shape[1]
    part = width + 1
    depth = q_ref.shape[0] // part

    def rims(z):
        b_ref[pl.ds(z * part, width), :] = zb_ref[z]
        a_ref[pl.ds(z * part, width), :] = za_ref[z]

    each(RIM, rims)

    def load(x):
        return jnp.concatenate(
            [
                b_ref[pl.ds(x, RIM, stride=part), :],
                q_ref[pl.ds(x, depth, stride=part), :],
                a_ref[pl.ds(x, RIM, stride=part), :],
            ],
            axis=0,
        )

    def store(x, value):
        r_ref[pl.ds(x, depth, stride=part), :] = value

    z_columns(load, mz_ref[...], width, store)

    def edges(z):
        first_ref[z] = r_ref[pl.ds(z * part, RIM), :]
        last_ref[z] = r_ref[pl.ds(z * part + width - RIM, RIM), :]

    each(depth, edges)


def back_xy_kernel(me_ref, w_ref, mx_ref, my_ref, r_ref, xl_ref, xr_ref, *rest):
    acc_ref, l_ref, mid_ref = rest if len(rest) == 3 else (None, *rest)
    me = me_ref[0]
    depth = xl_ref.shape[0]
    part = r_ref.shape[0] // depth

    def load(p):
        return jnp.concatenate(
            [xl_ref[p], r_ref[pl.ds(p * part, part - 1), :], xr_ref[p]], axis=0
        )

    def finish(p, back):
        term = w_ref[lax.div(p, 16)] * jnp.log(back)
        for quarter in range(4):
            slot = lax.rem(quarter - me + 4, 4)
            piece = term[quarter * 16 : quarter * 16 + 16]
            if acc_ref is not None:
                piece = piece + acc_ref[slot, p]
            l_ref[slot, p] = piece

    xy_planes(load, mx_ref[...], my_ref[...], depth, mid_ref, finish)


def assemble_kernel(at_ref, *refs):
    *pieces, block_ref, first_ref, last_ref, low_ref, high_ref = refs
    depth, narrow = pieces[0].shape[0], pieces[0].shape[1]
    for number, piece in enumerate(pieces):
        at = pl.multiple_of(at_ref[number], narrow)

        def step(z):
            block_ref[z, pl.ds(at, narrow), :] = piece[z]

        each(depth, step)
    first_ref[...] = block_ref[:RIM]
    last_ref[...] = block_ref[depth - RIM :]
    width = block_ref.shape[1]
    low_ref[...] = block_ref[:, :RIM]
    high_ref[...] = block_ref[:, width - RIM :]


def stack_kernel(at_ref, *refs):
    *pieces, block_ref = refs
    for number, piece in enumerate(pieces):
        block_ref[pl.ds(at_ref[number], piece.shape[0])] = piece[...]


def turn_kernel(at_ref, *refs):
    *pieces, out_ref, rows_ref = refs
    slab, columns = out_ref.shape[0], out_ref.shape[2]
    narrow = pieces[0].shape[1]
    width = narrow * len(pieces)
    count = columns // width
    starts = [pl.multiple_of(at_ref[number], narrow) for number in range(len(pieces))]

    def step(z, _):
        for number, piece in enumerate(pieces):
            for g in range(count):
                rows_ref[pl.ds(g * width + starts[number], narrow), :] = piece[z * count + g]
        out_ref[z] = rows_ref[...].T
        return 0

    lax.fori_loop(0, slab, step, 0)


VMEM = pl.BlockSpec(memory_space=pltpu.VMEM)
SMEM = pl.BlockSpec(memory_space=pltpu.SMEM)


def params(mebibytes):
    return pltpu.CompilerParams(vmem_limit_bytes=mebibytes * 2**20)


def forward(mz, mx, my, f, zb, za, xl, xr, cl, cr, obs):
    depth, width, lines = f.shape
    rim = jax.ShapeDtypeStruct((RIM, width, lines), F32)
    pitch = width + 2 * RIM + 1
    return pl.pallas_call(
        forward_kernel,
        in_specs=[VMEM] * 11,
        out_specs=[VMEM] * 3,
        out_shape=[jax.ShapeDtypeStruct((depth * (width + 1), lines), F32), rim, rim],
        scratch_shapes=[
            pltpu.VMEM(((depth + 2 * RIM) * pitch, lines), F32),
            pltpu.VMEM((depth * pitch, lines), F32),
            pltpu.VMEM((2, 2 * UNROLL * width, lines), F32),
        ],
        compiler_params=params(20),
        cost_estimate=pl.CostEstimate(flops=10**10, bytes_accessed=2 * 10**7, transcendentals=0),
        name="forward",
    )(mz, mx, my, f, zb, za, xl, xr, cl, cr, obs)


def back_z(mz, q, zb, za):
    width, lines = zb.shape[1:]
    depth = q.shape[0] // (width + 1)
    rim = jax.ShapeDtypeStruct((depth, RIM, lines), F32)
    padded = pltpu.VMEM((RIM * (width + 1), lines), F32)
    return pl.pallas_call(
        back_z_kernel,
        in_specs=[VMEM] * 4,
        out_specs=[VMEM] * 3,
        out_shape=[jax.ShapeDtypeStruct(q.shape, F32), rim, rim],
        scratch_shapes=[padded, padded],
        compiler_params=params(12),
        cost_estimate=pl.CostEstimate(flops=3 * 10**9, bytes_accessed=10**7, transcendentals=0),
        name="back_z",
    )(mz, q, zb, za)


def back_xy(me, weight, mx, my, r, xl, xr, acc=None):
    depth, _, lines = xl.shape
    width = r.shape[0] // depth - 1
    args = [me, weight, mx, my, r, xl, xr] + ([] if acc is None else [acc])
    return pl.pallas_call(
        back_xy_kernel,
        in_specs=[SMEM, SMEM] + [VMEM] * (len(args) - 2),
        out_specs=VMEM,
        out_shape=jax.ShapeDtypeStruct((4, depth, width // 4, lines), F32),
        scratch_shapes=[pltpu.VMEM((2, 2 * UNROLL * width, lines), F32)],
        compiler_params=params(12),
        cost_estimate=pl.CostEstimate(flops=5 * 10**9, bytes_accessed=10**7, transcendentals=10**6),
        name="back_xy",
    )(*args)


def assemble(at, pieces):
    depth, narrow, lines = pieces[0].shape
    width = narrow * len(pieces)
    rim = jax.ShapeDtypeStruct((RIM, width, lines), F32)
    side = jax.ShapeDtypeStruct((depth, RIM, lines), F32)
    return pl.pallas_call(
        assemble_kernel,
        in_specs=[SMEM] + [VMEM] * len(pieces),
        out_specs=[VMEM] * 5,
        out_shape=[jax.ShapeDtypeStruct((depth, width, lines), F32), rim, rim, side, side],
        compiler_params=params(16),
        cost_estimate=pl.CostEstimate(flops=10**6, bytes_accessed=10**7, transcendentals=0),
        name="assemble",
    )(at.astype(jnp.int32), *pieces)


def stack(at, pieces):
    slab, width, lines = pieces[0].shape
    return pl.pallas_call(
        stack_kernel,
        in_specs=[SMEM] + [VMEM] * len(pieces),
        out_specs=VMEM,
        out_shape=jax.ShapeDtypeStruct((slab * len(pieces), width, lines), F32),
        compiler_params=params(16),
        cost_estimate=pl.CostEstimate(flops=10**6, bytes_accessed=10**7, transcendentals=0),
        name="stack",
    )(at.astype(jnp.int32), *pieces)


def turn(at, pieces, slab):
    rows, narrow, lines = pieces[0].shape
    columns = rows // slab * narrow * len(pieces)
    return pl.pallas_call(
        turn_kernel,
        in_specs=[SMEM] + [VMEM] * len(pieces),
        out_specs=VMEM,
        out_shape=jax.ShapeDtypeStruct((slab, lines, columns), F32),
        scratch_shapes=[pltpu.VMEM((columns, lines), F32)],
        compiler_params=params(16),
        name="turn",
    )(at.astype(jnp.int32), *pieces)


def gather_quarters(quarter, half):
    below = lax.ppermute(quarter, "view", V_UP)
    above = lax.ppermute(quarter, "view", V_DOWN)
    first = lax.ppermute(below[:half], "view", V_UP)
    second = lax.ppermute(above[half:], "view", V_DOWN)
    return quarter, above, jnp.concatenate([first, second], axis=0), below


def scatter_quarters(parts):
    half = parts.shape[1] // 2
    first = lax.ppermute(parts[2, :half], "view", V_UP)
    second = lax.ppermute(parts[2, half:], "view", V_DOWN)
    up = jnp.concatenate([parts[1, :half] + first, parts[1, half:]], axis=0)
    down = jnp.concatenate([parts[3, :half], parts[3, half:] + second], axis=0)
    return parts[0] + lax.ppermute(up, "view", V_UP) + lax.ppermute(down, "view", V_DOWN)


def to_blocks(value):
    return lax.all_to_all(
        value, "owner", split_axis=1, concat_axis=0, axis_index_groups=GROUPS, tiled=True
    )


def z_rims(first, last):
    before = lax.ppermute(last, "owner", Z_UP)
    after = lax.ppermute(first, "owner", Z_DOWN)
    return before, after


def x_rims(first, last):
    left = lax.ppermute(last, "owner", X_UP)
    right = lax.ppermute(first, "owner", X_DOWN)
    return left, right


def local(estimate, axial_views, lateral_views, psf_axial, psf_lateral, coverage):
    slab, lines, columns = estimate.shape
    owner = lax.axis_index("owner")
    me = lax.axis_index("view")
    k = owner % 8
    z_chip = owner // 8
    width = columns // COLS
    depth = 8 * slab

    turned = estimate.transpose(0, 2, 1).reshape(slab, COLS, 4, width // 4, lines)
    mine = lax.dynamic_index_in_dim(turned, me, 2, keepdims=False)
    cover = jnp.repeat(coverage[0].astype(F32), 2, axis=0)
    cover = jnp.pad(cover[:, None, :], ((0, 0), (0, width // 4 - 1), (0, lines - cover.shape[1])))
    mine = jnp.concatenate([mine, cover[None]], axis=0).reshape(slab + 1, -1, lines)
    lateral_views, mine = lax.optimization_barrier((lateral_views, mine))
    got = to_blocks(mine).reshape(8, slab + 1, width // 4, lines)

    chunks = lateral_views[0].transpose(2, 0, 1).reshape(4, depth, slab, lines)
    pieces, places = [], []
    for t in range(4):
        target = (owner % 4 + t + z_chip) % 4
        pieces.append(lax.dynamic_index_in_dim(chunks, target, 0, keepdims=False))
        places.append(((z_chip - t - k // 2) % 4) * slab)
    axial_views, got, *pieces = lax.optimization_barrier((axial_views, got, *pieces))
    quarter = got[:, :slab].reshape(depth, width // 4, lines)
    cover = got[:, slab, 0, :8]
    pieces = [
        lax.ppermute(piece, "owner", lateral_round(t)) for t, piece in enumerate(pieces)
    ]
    axial_chunks = axial_views[0].transpose(0, 2, 1).reshape(slab, COLS, width, lines)
    axial_chunks = axial_chunks.transpose(1, 0, 2, 3)
    slabs = [
        lax.dynamic_index_in_dim(axial_chunks, (k + d) % 8, 0, keepdims=False) for d in range(8)
    ]
    slabs = [
        lax.ppermute(piece, "owner", axial_round(d)) if d else piece
        for d, piece in enumerate(slabs)
    ]
    lateral = assemble(jnp.stack(places), pieces)[0]

    count = jnp.sum(cover, axis=-1)
    weight_axial = lax.dynamic_index_in_dim(cover, me, 1, keepdims=False)
    weight_lateral = lax.dynamic_index_in_dim(cover, VA + me, 1, keepdims=False)

    taps = jnp.concatenate([psf_axial, psf_lateral], axis=0)
    taps = taps / jnp.sum(taps, axis=-1, keepdims=True)
    flipped = taps[..., ::-1]
    z_at = z_chip * depth + jnp.arange(depth)
    x_at = k * width + jnp.arange(width)
    y_at = jnp.arange(lines)
    ahead_z = left_form(band(taps[:, 0], depth, True))
    ahead_x = left_form(band(taps[:, 2], width, True))
    ahead_y = right_form(jnp.swapaxes(band(taps[:, 1], lines, False), 1, 2))
    wz = edge_weights(flipped[:, 0], z_at, 4 * depth)
    wx = edge_weights(flipped[:, 2], x_at, columns)
    wy = edge_weights(flipped[:, 1], y_at, lines)
    back_mz = left_form(band(flipped[:, 0], depth, True) / wz[:, :, None])
    back_mx = left_form(band(flipped[:, 2], width, True) / wx[:, :, None])
    back_my = right_form(
        jnp.swapaxes(band(flipped[:, 1], lines, False) / wy[:, :, None], 1, 2)
    )
    me_arr = me[None].astype(jnp.int32)

    for iteration in range(ITERS):
        pieces = gather_quarters(quarter, depth // 2)
        places = ((me + jnp.arange(4)) % 4) * (width // 4)
        block, first, last, low, high = assemble(places, pieces)
        before, after = z_rims(first, last)
        left, right = x_rims(low, high)
        corner_left, corner_right = x_rims(
            jnp.concatenate([before[:, :RIM], after[:, :RIM]], axis=0),
            jnp.concatenate([before[:, -RIM:], after[:, -RIM:]], axis=0),
        )
        logs = None
        for number, weight in ((1, weight_lateral), (0, weight_axial)):
            if number:
                obs = lateral
            elif iteration:
                obs = axial
            else:
                slabs, _ = lax.optimization_barrier((slabs, quotient))
                obs = axial = stack((k - jnp.arange(8)) % 8 * slab, slabs)
            quotient, first, last = forward(
                ahead_z[number], ahead_x[number], ahead_y[number],
                block, before, after, left, right, corner_left, corner_right, obs,
            )
            rz, low, high = back_z(back_mz[number], quotient, *z_rims(first, last))
            logs = back_xy(
                me_arr, weight, back_mx[number], back_my[number],
                rz, *x_rims(low, high), acc=logs,
            )
        total = scatter_quarters(logs)
        slabs = total.reshape(8, slab, width // 4, lines) / count[:, None, None, None]
        quarter = quarter * jnp.exp(slabs.reshape(quarter.shape))

    slabs = lax.all_to_all(
        quarter, "owner", split_axis=0, concat_axis=1, axis_index_groups=GROUPS, tiled=True
    )
    pieces = gather_quarters(slabs, slab // 2)
    pieces = [piece.reshape(slab * COLS, width // 4, lines) for piece in pieces]
    return turn(((me + jnp.arange(4)) % 4) * (width // 4), pieces, slab)


def solution(mesh):
    in_specs = (
        P("owner", None, None),
        P("view", "owner", None, None),
        P("view", "owner", None, None),
        P("view", None, None),
        P("view", None, None),
        P("owner", None, None),
    )
    out_specs = P("owner", None, None)
    return jax.shard_map(local, mesh=mesh, in_specs=in_specs, out_specs=out_specs, check_vma=False)
```
